512 devices in a mesh: cell: 64 (over z, y_lo, core), coef: 8 (over y_hi, x).
Axes of the slice: x: 4, y: 4 (y_hi: 2, y_lo: 2; y = y_hi * 2 + y_lo), z: 16, core: 2. Of those that a mesh axis runs over, the one named last changes fastest.
Arguments:
- multipoles: bfloat16 [4096, 9, 1024], P('cell', None, 'coef'), may hold values from -6 to 6
- rotation: bfloat16 [4, 8, 128, 128], P(None, 'coef')
- coaxial: bfloat16 [40, 8, 128, 128], P(None, 'coef')
- offsets: int32 [40], replicated, may hold values from -128 to 128, as said below
- class_index: int32 [40], replicated, may hold values from 0 to 3, as said below
Outputs:
- local_field: bfloat16 [4096, 9, 1024], P('cell', None, 'coef')
The draws below stay inside these ranges and needn't reach their ends.
Inputs may be any that keep to these rules, and one draw needn't show every extreme that they name: The offsets are distinct and nonzero, and both 128 and -128 occur. `class_index`: each class is named by exactly 10 offsets.
All inputs are finite; a program needn't handle non-finite values.
Results may differ from the reference program's by a relative error of at most 0.0057.
Values may be sent and summed in bfloat16 or wider, within the bound.
A program may use at most 64 MiB of HBM per device.

```python
import math
import jax
import jax.numpy as jnp
import numpy as np
from jax import lax

COEFS = 1024
COMPONENTS = 9
K = 40
NCLASS = 4
PER = 10
REACH = 128
CELLS = 4096


def level_scales():
    values = []
    for block_number in range(8):
        for level_value in (block_number, 15 - block_number, 16 + block_number, 31 - block_number):
            values.extend([1.0 / math.sqrt(2 * level_value + 1)] * (2 * level_value + 1))
    return np.array(values, dtype=np.float32).reshape(8, 128, 1)


def order_scales():
    values = []
    for block_number in range(8):
        if block_number == 0:
            magnitudes = (0, 16, 8, 24)
        else:
            magnitudes = (block_number, 32 - block_number, 16 - block_number, 16 + block_number)
        for size_m in magnitudes:
            copies = 1 if size_m == 0 else 2
            values.extend([1.0 / math.sqrt(32 - size_m)] * ((32 - size_m) * copies))
    return np.array(values, dtype=np.float32).reshape(8, 128, 1)


def unit_noise(key, shape):
    return jax.random.normal(key, shape, jnp.float32)


def draw_rotation(key, part):
    noise = unit_noise(jax.random.fold_in(key, 17), (NCLASS, 8, 128, 128))
    return (noise * jnp.asarray(level_scales())).astype(jnp.bfloat16)


def draw_coaxial(key, part):
    noise = unit_noise(jax.random.fold_in(key, 19), (K, 8, 128, 128))
    scaled = noise * jnp.asarray(order_scales()) / math.sqrt(K // NCLASS)
    return scaled.astype(jnp.bfloat16)


def draw_offsets(key, part):
    own_key = jax.random.fold_in(key, 11)
    inner = jnp.concatenate([jnp.arange(1 - REACH, 0, dtype=jnp.int32), jnp.arange(1, REACH, dtype=jnp.int32)])
    picked = jax.random.permutation(own_key, inner)[0:K - 2]
    ends = jnp.array([REACH, -REACH], dtype=jnp.int32)
    return jax.random.permutation(jax.random.fold_in(own_key, 7), jnp.concatenate([ends, picked])).astype(jnp.int32)


def draw_class_index(key, part):
    return (jax.random.permutation(jax.random.fold_in(key, 13), K) % NCLASS).astype(jnp.int32)


def block_levels(key, extent, cuts, smallest, high):
    def one(axis_at, blocks):
        heights = jax.random.uniform(jax.random.fold_in(jax.random.fold_in(key, 6), axis_at), (blocks,), jnp.float32, smallest / len(cuts), high / len(cuts))
        return jnp.repeat(jnp.exp(heights), extent[axis_at] // blocks).reshape((-1,) + (1,) * (len(extent) - axis_at - 1))

    level = one(*cuts[0])
    for cut in cuts[1:]:
        level = level * one(*cut)
    return level


def normal_values(key, shape, deviation, bound, shards=(), held_as=jnp.bfloat16):
    level = block_levels(key, shape, shards, -0.22, 0.18) if shards else 1.0
    result = jax.random.normal(key, shape, jnp.float32) * deviation * level
    return jnp.minimum(jnp.maximum(result, -bound), bound).astype(held_as)


def setup_inputs(seed: int = 0) -> dict:
    streams_of = jax.random.split(jax.random.key(seed), 6)
    return {
        "multipoles": normal_values(streams_of[0], (CELLS, COMPONENTS, COEFS), 1.0, 6.0, ((0, 64), (2, 8))),
        "rotation": draw_rotation(jax.random.fold_in(streams_of[5], 71), 0),
        "coaxial": draw_coaxial(jax.random.fold_in(streams_of[5], 71), 0),
        "offsets": draw_offsets(jax.random.fold_in(streams_of[5], 71), 0),
        "class_index": draw_class_index(jax.random.fold_in(streams_of[5], 71), 0),
    }


def layout_tables():
    degree_list = []
    for block_number in range(8):
        for level_value in (block_number, 15 - block_number, 16 + block_number, 31 - block_number):
            for order_value in range(-level_value, level_value + 1):
                degree_list.append((level_value, order_value))
    order_list = []
    for block_number in range(8):
        if block_number == 0:
            magnitudes = (0, 16, 8, 24)
        else:
            magnitudes = (block_number, 32 - block_number, 16 - block_number, 16 + block_number)
        for size_m in magnitudes:
            signed_list = [size_m] if size_m == 0 else [size_m, -size_m]
            for order_value in signed_list:
                for level_value in range(size_m, 32):
                    order_list.append((level_value, order_value))
    position = {}
    for entry_index, entry_pair in enumerate(degree_list):
        position[entry_pair] = entry_index
    to_orders = np.array([position[entry_pair] for entry_pair in order_list], dtype=np.int32)
    to_degrees = np.argsort(to_orders).astype(np.int32)
    levels = np.array([entry_pair[0] for entry_pair in degree_list]).reshape(8, 128)
    orders = np.array([entry_pair[1] for entry_pair in order_list]).reshape(8, 128)
    same_level = (levels[:, :, None] == levels[:, None, :]).astype(np.float32)
    same_order = (orders[:, :, None] == orders[:, None, :]).astype(np.float32)
    return to_orders, to_degrees, same_level, same_order


def reference(multipoles, rotation, coaxial, offsets, class_index):
    to_orders, to_degrees, same_level, same_order = layout_tables()
    rotation_full = rotation.astype(jnp.float32) * jnp.asarray(same_level, jnp.float32)
    coaxial_full = coaxial.astype(jnp.float32) * jnp.asarray(same_order, jnp.float32)
    cell_total = multipoles.shape[0]
    source = multipoles.astype(jnp.float32).reshape(cell_total, 9, 8, 128)
    grouped = jnp.argsort(class_index, stable=True).astype(jnp.int32).reshape(NCLASS, PER)
    field_sum = jnp.zeros((cell_total, 9, 8, 128), jnp.float32)
    for class_number in range(NCLASS):
        turned = jnp.einsum("tsgj,gij->tsgi", source, rotation_full[class_number]).astype(jnp.bfloat16)
        turned = lax.optimization_barrier(turned)
        aligned = turned.reshape(cell_total, 9, 1024)[:, :, to_orders].astype(jnp.float32)
        doubled = jnp.concatenate([aligned, aligned], axis=0)

        def add_offset(position_index, carried, class_number=class_number, doubled=doubled):
            chosen = grouped[class_number, position_index]
            start_cell = ((offsets[chosen] + cell_total) % cell_total).astype(jnp.int32)
            shifted = lax.dynamic_slice_in_dim(doubled, start_cell, cell_total, 0).reshape(cell_total, 9, 8, 128)
            matrix = lax.dynamic_index_in_dim(coaxial_full, chosen, 0, keepdims=False)
            return carried + jnp.einsum("tsgj,gij->tsgi", shifted, matrix)

        translated = lax.fori_loop(0, PER, add_offset, jnp.zeros((cell_total, 9, 8, 128), jnp.float32))
        rounded = lax.optimization_barrier(translated.astype(jnp.bfloat16))
        returned = rounded.reshape(cell_total, 9, 1024)[:, :, to_degrees].astype(jnp.float32).reshape(cell_total, 9, 8, 128)
        field_sum = field_sum + jnp.einsum("tsgi,gij->tsgj", returned, rotation_full[class_number])
    return field_sum.reshape(cell_total, 9, 1024).astype(jnp.bfloat16)
```

```python
import functools

import jax
import jax.numpy as jnp
import numpy as np
from jax import lax
from jax.experimental import pallas as pl
from jax.experimental.pallas import tpu as pltpu
from jax.sharding import PartitionSpec as P

NCLASS = 4
PER = 10
COMPONENTS = 9
CHUNKS = ((0, 4), (4, 9))
MESH = pl.DeviceIdType.MESH


def block_tables():
    degree_list = []
    for block_number in range(8):
        for level in (block_number, 15 - block_number, 16 + block_number, 31 - block_number):
            for order in range(-level, level + 1):
                degree_list.append((level, order))
    order_list = []
    for block_number in range(8):
        if block_number == 0:
            magnitudes = (0, 16, 8, 24)
        else:
            magnitudes = (block_number, 32 - block_number, 16 - block_number, 16 + block_number)
        for size_m in magnitudes:
            for order in [size_m] if size_m == 0 else [size_m, -size_m]:
                for level in range(size_m, 32):
                    order_list.append((level, order))
    where_degree = {pair: index for index, pair in enumerate(degree_list)}
    by_degree = np.zeros((8, 128, 128), np.float32)
    by_order = np.zeros((8, 128, 128), np.float32)
    filled = np.zeros((8, 8), np.int32)
    for order_at, pair in enumerate(order_list):
        degree_at = where_degree[pair]
        a, b = degree_at // 128, order_at // 128
        slot = filled[a, b]
        filled[a, b] += 1
        by_degree[a, b * 16 + slot, degree_at % 128] = 1.0
        by_order[b, a * 16 + slot, order_at % 128] = 1.0
    assert (filled == 16).all()
    levels = np.array([pair[0] for pair in degree_list]).reshape(8, 128)
    orders = np.array([pair[1] for pair in order_list]).reshape(8, 128)
    same_level = (levels[:, :, None] == levels[:, None, :]).astype(np.float32)
    same_order = (orders[:, :, None] == orders[:, None, :]).astype(np.float32)
    return np.stack([by_degree, by_order, same_level, same_order], axis=1)


def pairs_of(first, last):
    return [tuple(range(s, min(s + 2, last))) for s in range(first, last, 2)]


def nt(left, right):
    return lax.dot_general(left, right, (((1,), (1,)), ((), ())), preferred_element_type=jnp.float32)


def nn(left, right):
    return jnp.dot(left, right, preferred_element_type=jnp.float32)


def kernel(x_ref, tables_hbm, rot_hbm, coax_hbm, offs_ref, cls_ref, out_ref, *scratch):
    count = len(CHUNKS)
    turned = scratch[0:count]
    got = scratch[count:2 * count]
    below = scratch[2 * count:3 * count]
    above = scratch[3 * count:4 * count]
    moved = scratch[4 * count:5 * count]
    back = scratch[5 * count:6 * count]
    (cells, tables, rot, coax, turning, turning_t, steps, chosen,
     load_sem, fwd_send, fwd_recv, halo_send, halo_recv, bwd_send, bwd_recv) = scratch[6 * count:]
    cell = lax.axis_index("cell")
    coef = lax.axis_index("coef")
    cell_total = lax.axis_size("cell")
    part = cell % 4
    plane = cell - part
    me = part * 8 + coef
    up = (cell + 4) % cell_total
    down = (cell + cell_total - 4) % cell_total

    def partner(i):
        other = (me + i) % 32
        return other, (plane + other // 8, other % 8)

    barrier = pltpu.get_barrier_semaphore()

    def greet(i, carry):
        pl.semaphore_signal(barrier, inc=1, device_id=partner(i)[1], device_id_type=MESH)
        return carry

    lax.fori_loop(1, 32, greet, 0)
    pl.semaphore_signal(barrier, inc=1, device_id=(up, coef), device_id_type=MESH)
    pl.semaphore_signal(barrier, inc=1, device_id=(down, coef), device_id_type=MESH)

    loads = [
        pltpu.make_async_copy(tables_hbm.at[coef], tables, load_sem.at[0]),
        pltpu.make_async_copy(rot_hbm, rot, load_sem.at[1]),
        pltpu.make_async_copy(coax_hbm, coax, load_sem.at[2]),
    ]
    for load in loads:
        load.start()
    loads[0].wait()
    loads[1].wait()
    for c in range(NCLASS):
        masked = rot[c, 0] * tables[2]
        turning[pl.ds(c * 128, 128), :] = nn(tables[0], masked).astype(jnp.bfloat16)

    def spread(source, target, send_sem, recv_sem):
        def one(i, carry):
            other, device = partner(i)
            pltpu.make_async_remote_copy(
                source.at[other], target.at[me], send_sem, recv_sem,
                device_id=device, device_id_type=MESH).start()
            return carry

        lax.fori_loop(1, 32, one, 0)
        pltpu.make_async_copy(source.at[me], target.at[me], recv_sem).start()

    for g, (first, last) in enumerate(CHUNKS):
        rows = x_ref[first:last].reshape((last - first) * 64, 128)
        result = nt(turning[...], rows).astype(jnp.bfloat16)
        turned[g][...] = result.reshape(32, 16, (last - first) * 64)
        if g == 0:
            pl.semaphore_wait(barrier, 33)
        spread(turned[g], got[g], fwd_send.at[g], fwd_recv.at[g])

    def pick(k, carry):
        seen, kept = carry[0], carry[1:]
        hit = cls_ref[k] == part
        kept = tuple(
            jnp.where(jnp.logical_and(hit, seen == p), k, old) for p, old in enumerate(kept))
        return (seen + jnp.where(hit, 1, 0),) + kept

    picked = lax.fori_loop(0, NCLASS * PER, pick, (jnp.int32(0),) * (PER + 1))[1:]
    for p in range(PER):
        chosen[p] = picked[p]
    loads[2].wait()

    def prepare(p, carry):
        masked = coax[chosen[p], 0] * tables[3]
        half = nn(tables[1], masked).astype(jnp.bfloat16)
        steps[p] = nt(half, tables[1]).astype(jnp.bfloat16)
        return carry

    lax.fori_loop(0, PER, prepare, 0)
    for c in range(NCLASS):
        piece = turning[pl.ds(c * 128, 128), :].astype(jnp.float32)
        turning_t[:, c * 128:(c + 1) * 128] = piece.T.astype(jnp.bfloat16)

    def lay(buffer, row, groups, g):
        first, last = CHUNKS[g]
        for j in range(groups):
            block = buffer[j * 8:(j + 1) * 8].reshape(128, (last - first) * 64)
            for at, s in enumerate(range(first, last, 2)):
                n = min(2, last - s)
                piece = block[:, at * 128:at * 128 + n * 64].astype(jnp.float32).T
                for m in range(n):
                    cells[s + m, row + j * 64:row + j * 64 + 64, :] = piece[m * 64:(m + 1) * 64]

    def arrive(g):
        pltpu.make_async_copy(got[g], got[g], fwd_recv.at[g]).wait()
        pltpu.make_async_remote_copy(
            got[g].at[pl.ds(16, 16)], below[g], halo_send.at[g, 0], halo_recv.at[g, 0],
            device_id=(up, coef), device_id_type=MESH).start()
        pltpu.make_async_remote_copy(
            got[g].at[pl.ds(0, 16)], above[g], halo_send.at[g, 1], halo_recv.at[g, 1],
            device_id=(down, coef), device_id_type=MESH).start()
        lay(got[g], 128, 4, g)

    def translate(g):
        first, last = CHUNKS[g]
        pltpu.make_async_copy(below[g], below[g], halo_recv.at[g, 0]).wait()
        lay(below[g], 0, 2, g)
        pltpu.make_async_copy(above[g], above[g], halo_recv.at[g, 1]).wait()
        lay(above[g], 384, 2, g)
        matrices = jnp.concatenate([steps[p] for p in range(PER)], axis=1)
        starts = [128 + offs_ref[chosen[p]] for p in range(PER)]
        for at, members in enumerate(pairs_of(first, last)):
            width = 64 * len(members)
            for j in range(0, 4, 2):
                pieces = []
                for p in range(PER):
                    pieces.append(jnp.concatenate(
                        [cells[s, pl.ds(starts[p] + i * 64, 64), :] for i in (j, j + 1) for s in members],
                        axis=0).astype(jnp.bfloat16))
                result = nt(matrices, jnp.concatenate(pieces, axis=1)).astype(jnp.bfloat16)
                for i in range(2):
                    moved[g][(j + i) * 8:(j + i + 1) * 8, :, at * 128:at * 128 + width] = (
                        result[:, i * width:(i + 1) * width].reshape(8, 16, width))
        spread(moved[g], back[g], bwd_send.at[g], bwd_recv.at[g])

    for g in range(count + 1):
        if g < count:
            arrive(g)
        if g > 0:
            translate(g - 1)

    for g, (first, last) in enumerate(CHUNKS):
        pltpu.make_async_copy(back[g], back[g], bwd_recv.at[g]).wait()
        block = back[g][...].reshape(512, (last - first) * 64)
        field = nn(turning_t[...], block)
        for at, members in enumerate(pairs_of(first, last)):
            piece = field[:, at * 128:at * 128 + 64 * len(members)].T.astype(jnp.bfloat16)
            for m, s in enumerate(members):
                out_ref[s] = piece[m * 64:(m + 1) * 64]

    for g in range(count):
        sent = turned[g].at[pl.ds(0, 31)]
        pltpu.make_async_copy(sent, sent, fwd_send.at[g]).wait()
        pltpu.make_async_copy(below[g], below[g], halo_send.at[g, 0]).wait()
        pltpu.make_async_copy(above[g], above[g], halo_send.at[g, 1]).wait()
        sent = moved[g].at[pl.ds(0, 31)]
        pltpu.make_async_copy(sent, sent, bwd_send.at[g]).wait()


def on_device(multipoles, rotation, coaxial, offsets, class_index):
    tables = jnp.asarray(block_tables(), jnp.bfloat16)
    rows = jnp.transpose(multipoles, (1, 0, 2))
    vmem = pl.BlockSpec(memory_space=pltpu.VMEM)
    smem = pl.BlockSpec(memory_space=pltpu.SMEM)
    hbm = pl.BlockSpec(memory_space=pl.ANY)
    count = len(CHUNKS)
    widths = [64 * (last - first) for first, last in CHUNKS]
    bf16 = jnp.bfloat16
    scratch = []
    for parts in (32, 32, 16, 16, 32, 32):
        scratch += [pltpu.VMEM((parts, 16, width), bf16) for width in widths]
    scratch += [
        pltpu.VMEM((COMPONENTS, 512, 128), jnp.float32),
        pltpu.VMEM((4, 128, 128), bf16),
        pltpu.VMEM((NCLASS, 1, 128, 128), bf16),
        pltpu.VMEM((NCLASS * PER, 1, 128, 128), bf16),
        pltpu.VMEM((NCLASS * 128, 128), bf16),
        pltpu.VMEM((128, NCLASS * 128), bf16),
        pltpu.VMEM((PER, 128, 128), bf16),
        pltpu.SMEM((PER,), jnp.int32),
        pltpu.SemaphoreType.DMA((3,)),
        pltpu.SemaphoreType.DMA((count,)),
        pltpu.SemaphoreType.DMA((count,)),
        pltpu.SemaphoreType.DMA((count, 2)),
        pltpu.SemaphoreType.DMA((count, 2)),
        pltpu.SemaphoreType.DMA((count,)),
        pltpu.SemaphoreType.DMA((count,)),
    ]
    field = pl.pallas_call(
        kernel,
        out_shape=jax.ShapeDtypeStruct((COMPONENTS, 64, 128), bf16),
        in_specs=[vmem, hbm, hbm, hbm, smem, smem],
        out_specs=vmem,
        scratch_shapes=scratch,
        compiler_params=pltpu.CompilerParams(collective_id=0, has_side_effects=True),
        name="multipole_to_local",
    )(rows, tables, rotation, coaxial, offsets, class_index)
    return jnp.transpose(field, (1, 0, 2))


def solution(mesh):
    placed = (
        P("cell", None, "coef"),
        P(None, "coef", None, None),
        P(None, "coef", None, None),
        P(),
        P(),
    )
    return jax.shard_map(
        on_device, mesh=mesh, in_specs=placed, out_specs=P("cell", None, "coef"), check_vma=False
    )
```

```python
import jax
import jax.numpy as jnp
import numpy as np
from jax import lax
from jax.experimental import pallas as pl
from jax.experimental.pallas import tpu as pltpu
from jax.sharding import PartitionSpec as P

NCLASS = 4
PER = 10
COMPONENTS = 9
CHUNKS = ((0, 2), (2, 4), (4, 6), (6, 8), (8, 9))
MESH = pl.DeviceIdType.MESH


def block_tables():
    degree_list = []
    for block_number in range(8):
        for level in (block_number, 15 - block_number, 16 + block_number, 31 - block_number):
            for order in range(-level, level + 1):
                degree_list.append((level, order))
    order_list = []
    for block_number in range(8):
        if block_number == 0:
            magnitudes = (0, 16, 8, 24)
        else:
            magnitudes = (block_number, 32 - block_number, 16 - block_number, 16 + block_number)
        for size_m in magnitudes:
            for order in [size_m] if size_m == 0 else [size_m, -size_m]:
                for level in range(size_m, 32):
                    order_list.append((level, order))
    where_degree = {pair: index for index, pair in enumerate(degree_list)}
    by_degree = np.zeros((8, 128, 128), np.float32)
    by_order = np.zeros((8, 128, 128), np.float32)
    filled = np.zeros((8, 8), np.int32)
    for order_at, pair in enumerate(order_list):
        degree_at = where_degree[pair]
        a, b = degree_at // 128, order_at // 128
        slot = filled[a, b]
        filled[a, b] += 1
        by_degree[a, b * 16 + slot, degree_at % 128] = 1.0
        by_order[b, (slot // 8) * 64 + a * 8 + slot % 8, order_at % 128] = 1.0
    assert (filled == 16).all()
    levels = np.array([pair[0] for pair in degree_list]).reshape(8, 128)
    orders = np.array([pair[1] for pair in order_list]).reshape(8, 128)
    same_level = (levels[:, :, None] == levels[:, None, :]).astype(np.float32)
    same_order = (orders[:, :, None] == orders[:, None, :]).astype(np.float32)
    return np.stack([by_degree, by_order, same_level, same_order], axis=1)


def packed(g):
    return CHUNKS[g][1] - CHUNKS[g][0] == 1


def depth(g):
    return 8 if packed(g) else 16


def lanes(g):
    return max(128, 64 * (CHUNKS[g][1] - CHUNKS[g][0]))


def nt(left, right):
    return lax.dot_general(left, right, (((1,), (1,)), ((), ())), preferred_element_type=jnp.float32)


def nn(left, right):
    return jnp.dot(left, right, preferred_element_type=jnp.float32)


def halves_first(rows):
    count, width = rows.shape[0] // 16, rows.shape[1]
    split = rows.reshape(count, 2, 8, width)
    return jnp.concatenate([split[:, h].reshape(count * 8, width) for h in range(2)], axis=0)


def halves_last(rows):
    count, width = rows.shape[0] // 16, rows.shape[1]
    split = rows.reshape(2, count, 8, width)
    pieces = [split[h, n] for n in range(count) for h in range(2)]
    return jnp.concatenate(pieces, axis=0)


def kernel(x_hbm, tables_hbm, rot_hbm, coax_hbm, offs_ref, cls_ref, out_ref, *scratch):
    count = len(CHUNKS)
    names = ("turned", "middle", "got", "below", "above", "moved", "between", "back")
    buffers = {name: scratch[i * count:(i + 1) * count] for i, name in enumerate(names)}
    turned, middle, got, below, above, moved, between, back = (buffers[name] for name in names)
    (x_ref, cells, tables, rot, coax, turning, turning_t, steps, chosen, load_sem,
     fx_send, fx_recv, fy_send, fy_recv, halo_send, halo_recv,
     bx_send, bx_recv, by_send, by_recv) = scratch[len(names) * count:]
    cell = lax.axis_index("cell")
    coef = lax.axis_index("coef")
    cell_total = lax.axis_size("cell")
    part = cell % 4
    plane = cell - part
    along = coef % 4
    high = coef // 4
    column = part * 2 + high
    up = (cell + 4) % cell_total
    down = (cell + cell_total - 4) % cell_total

    def along_device(i):
        other = (along + i) % 4
        return other, (cell, high * 4 + other)

    def column_device(i):
        other = (column + i) % 8
        return other, (plane + other // 2, (other % 2) * 4 + along)

    def half_device(half, i):
        other = half * 4 + (column + i) % 4
        return other, (plane + other // 2, (other % 2) * 4 + along)

    barrier = pltpu.get_barrier_semaphore()
    friends = [along_device(i)[1] for i in range(1, 4)] + [column_device(i)[1] for i in range(1, 8)]
    friends += [(up, coef), (down, coef)]
    for device in friends:
        pl.semaphore_signal(barrier, inc=1, device_id=device, device_id_type=MESH)

    loads = [
        pltpu.make_async_copy(tables_hbm.at[coef], tables, load_sem.at[0]),
        pltpu.make_async_copy(rot_hbm, rot, load_sem.at[1]),
        pltpu.make_async_copy(coax_hbm, coax, load_sem.at[2]),
        pltpu.make_async_copy(x_hbm, x_ref, load_sem.at[3]),
    ]
    for load in (loads[0], loads[1], loads[3], loads[2]):
        load.start()
    loads[0].wait()
    loads[1].wait()
    for c in range(NCLASS):
        masked = rot[c, 0] * tables[2]
        rows = nn(tables[0], masked).astype(jnp.bfloat16)
        for b in range(8):
            at = ((b % 4) * 8 + c * 2 + b // 4) * 16
            turning[at:at + 16, :] = rows[b * 16:(b + 1) * 16]

    def send(source, target, send_sem, recv_sem, device):
        pltpu.make_async_remote_copy(
            source, target, send_sem, recv_sem, device_id=device, device_id_type=MESH).start()

    def landed(ref, sem):
        pltpu.make_async_copy(ref, ref, sem).wait()

    loads[3].wait()
    for g, (first, last) in enumerate(CHUNKS):
        rows = x_ref[first:last].reshape((last - first) * 64, 128)
        if packed(g):
            matrix = halves_first(turning[...].astype(jnp.float32)).astype(jnp.bfloat16)
            result = nt(matrix, rows)
            result = jnp.concatenate([result[:256], result[256:]], axis=1)
        else:
            result = nt(turning[...], rows)
        turned[g][...] = result.astype(jnp.bfloat16).reshape(4, 8, depth(g), lanes(g))
        if g == 0:
            pl.semaphore_wait(barrier, len(friends))
        for i in range(1, 4):
            other, device = along_device(i)
            send(turned[g].at[other], middle[g].at[:, along], fx_send.at[g], fx_recv.at[g], device)
        pltpu.make_async_copy(
            turned[g].at[along], middle[g].at[:, along], fx_recv.at[g]).start()

    def pick(k, carry):
        seen, kept = carry[0], carry[1:]
        hit = cls_ref[k] == part
        kept = tuple(
            jnp.where(jnp.logical_and(hit, seen == p), k, old) for p, old in enumerate(kept))
        return (seen + jnp.where(hit, 1, 0),) + kept

    def forward(g):
        landed(middle[g], fx_recv.at[g])
        for i in range(1, 8):
            other, device = column_device(i)
            send(middle[g].at[other], got[g].at[column], fy_send.at[g], fy_recv.at[g], device)
        pltpu.make_async_copy(
            middle[g].at[column], got[g].at[column], fy_recv.at[g]).start()

    def prepare_steps():
        picked = lax.fori_loop(0, NCLASS * PER, pick, (jnp.int32(0),) * (PER + 1))[1:]
        for p in range(PER):
            chosen[p] = picked[p]
        loads[2].wait()

        def prepare(p, carry):
            masked = coax[chosen[p], 0] * tables[3]
            half = nn(tables[1], masked).astype(jnp.bfloat16)
            steps[p] = nt(half, tables[1]).astype(jnp.bfloat16)
            return carry

        lax.fori_loop(0, PER, prepare, 0)

    def prepare_return():
        pieces = []
        for c in range(NCLASS):
            for b in range(8):
                at = ((b % 4) * 8 + c * 2 + b // 4) * 16
                pieces.append(turning[at:at + 16, :])
        rows = jnp.concatenate(pieces, axis=0).astype(jnp.float32)
        for kind, matrix in enumerate((rows, halves_first(rows))):
            for c in range(NCLASS):
                turning_t[kind, :, c * 128:(c + 1) * 128] = (
                    matrix[c * 128:(c + 1) * 128].T.astype(jnp.bfloat16))

    def lay(buffer, row, groups, g):
        first, last = CHUNKS[g]
        for j in range(groups):
            block = buffer[j * 2:(j + 1) * 2].reshape(8 * depth(g), lanes(g))
            if packed(g):
                piece = block.astype(jnp.float32).T
                cells[first, row + j * 64:row + j * 64 + 64, :] = jnp.concatenate(
                    [piece[:64], piece[64:]], axis=1)
                continue
            for at in range(0, lanes(g), 128):
                piece = halves_first(block[:, at:at + 128].astype(jnp.float32)).T
                for m in range(2):
                    cells[first + at // 64 + m, row + j * 64:row + j * 64 + 64, :] = (
                        piece[m * 64:(m + 1) * 64])

    def arrive(g):
        landed(got[g], fy_recv.at[g])
        send(got[g].at[pl.ds(0, 4)], above[g], halo_send.at[g, 1], halo_recv.at[g, 1], (down, coef))
        send(got[g].at[pl.ds(4, 4)], below[g], halo_send.at[g, 0], halo_recv.at[g, 0], (up, coef))
        lay(got[g], 128, 4, g)

    def translate(g, half):
        first, last = CHUNKS[g]
        if half:
            landed(above[g], halo_recv.at[g, 1])
            lay(above[g], 384, 2, g)
        else:
            landed(below[g], halo_recv.at[g, 0])
            lay(below[g], 0, 2, g)
        matrices = jnp.concatenate([steps[p] for p in range(PER)], axis=1)
        starts = [128 + half * 128 + offs_ref[chosen[p]] for p in range(PER)]
        for at, s0 in enumerate(range(first, last, 2)):
            members = range(s0, min(s0 + 2, last))
            width = 64 * len(members)
            pieces = []
            for p in range(PER):
                pieces.append(jnp.concatenate(
                    [cells[s, pl.ds(starts[p] + i * 64, 64), :] for i in range(2) for s in members],
                    axis=0).astype(jnp.bfloat16))
            result = nt(matrices, jnp.concatenate(pieces, axis=1))
            for i in range(2):
                piece = result[:, i * width:(i + 1) * width]
                if packed(g):
                    piece = jnp.concatenate([piece[:64], piece[64:]], axis=1)
                else:
                    piece = halves_last(piece)
                piece = piece.astype(jnp.bfloat16).reshape(8, depth(g), 128)
                for a in range(8):
                    moved[g][a % 4, (half * 2 + i) * 2 + a // 4, :, at * 128:at * 128 + 128] = piece[a]
        span = pl.ds(half * 4, 4)
        for i in range(1, 4):
            other, device = along_device(i)
            send(moved[g].at[other, span], between[g].at[span, along],
                 bx_send.at[g, half], bx_recv.at[g, half], device)
        pltpu.make_async_copy(
            moved[g].at[along, span], between[g].at[span, along], bx_recv.at[g, half]).start()

    def onward(g, half):
        landed(between[g].at[pl.ds(half * 4, 4)], bx_recv.at[g, half])
        inside = column // 4 == half
        for i in range(4):
            other, device = half_device(half, i)
            if i:
                send(between[g].at[other], back[g].at[column], by_send.at[g, half], by_recv.at[g], device)
            else:
                @pl.when(jnp.logical_not(inside))
                def _():
                    send(between[g].at[other], back[g].at[column], by_send.at[g, half], by_recv.at[g], device)

                @pl.when(inside)
                def _():
                    pltpu.make_async_copy(
                        between[g].at[other], back[g].at[column], by_recv.at[g]).start()

    def finish(g):
        first, last = CHUNKS[g]
        landed(back[g], by_recv.at[g])
        block = back[g][...].reshape(32 * depth(g), lanes(g))
        if packed(g):
            block = jnp.concatenate([block[:, :64], block[:, 64:]], axis=0)
        matrix = turning_t[1 if packed(g) else 0]
        field = nn(matrix, block)
        for at, s0 in enumerate(range(first, last, 2)):
            members = range(s0, min(s0 + 2, last))
            piece = field[:, at * 128:at * 128 + 64 * len(members)].T.astype(jnp.bfloat16)
            for m, s in enumerate(members):
                out_ref[s] = piece[m * 64:(m + 1) * 64]

    forward(0)
    prepare_steps()
    prepare_return()
    for g in range(1, count + 2):
        if g < count:
            forward(g)
        if g - 1 < count:
            arrive(g - 1)
        if g >= 2:
            translate(g - 2, 1)
    onward(0, 1)
    for g in range(count):
        translate(g, 0)
        if g + 1 < count:
            onward(g + 1, 1)
        if g:
            onward(g - 1, 0)
    onward(count - 1, 0)
    for g in range(count):
        finish(g)

    for g in range(count):
        landed(turned[g].at[pl.ds(0, 3)], fx_send.at[g])
        landed(middle[g].at[pl.ds(0, 7)], fy_send.at[g])
        landed(below[g], halo_send.at[g, 0])
        landed(above[g], halo_send.at[g, 1])
        for half in range(2):
            landed(moved[g].at[pl.ds(0, 3), pl.ds(0, 4)], bx_send.at[g, half])

            @pl.when(column // 4 == half)
            def _():
                landed(between[g].at[pl.ds(0, 3)], by_send.at[g, half])

            @pl.when(column // 4 != half)
            def _():
                landed(between[g].at[pl.ds(0, 4)], by_send.at[g, half])


def on_device(multipoles, rotation, coaxial, offsets, class_index):
    tables = jnp.asarray(block_tables(), jnp.bfloat16)
    rows = jnp.transpose(multipoles, (1, 0, 2))
    vmem = pl.BlockSpec(memory_space=pltpu.VMEM)
    smem = pl.BlockSpec(memory_space=pltpu.SMEM)
    hbm = pl.BlockSpec(memory_space=pl.ANY)
    count = len(CHUNKS)
    bf16 = jnp.bfloat16
    scratch = []
    for outer in ((4, 8), (8, 4), (8, 4), (4, 4), (4, 4), (4, 8), (8, 4), (8, 4)):
        scratch += [pltpu.VMEM(outer + (depth(g), lanes(g)), bf16) for g in range(count)]
    dma = pltpu.SemaphoreType.DMA
    scratch += [
        pltpu.VMEM((COMPONENTS, 64, 128), bf16),
        pltpu.VMEM((COMPONENTS, 512, 128), jnp.float32),
        pltpu.VMEM((4, 128, 128), bf16),
        pltpu.VMEM((NCLASS, 1, 128, 128), bf16),
        pltpu.VMEM((NCLASS * PER, 1, 128, 128), bf16),
        pltpu.VMEM((NCLASS * 128, 128), bf16),
        pltpu.VMEM((2, 128, NCLASS * 128), bf16),
        pltpu.VMEM((PER, 128, 128), bf16),
        pltpu.SMEM((PER,), jnp.int32),
        dma((4,)),
        dma((count,)), dma((count,)), dma((count,)), dma((count,)),
        dma((count, 2)), dma((count, 2)),
        dma((count, 2)), dma((count, 2)), dma((count, 2)), dma((count,)),
    ]
    field = pl.pallas_call(
        kernel,
        out_shape=jax.ShapeDtypeStruct((COMPONENTS, 64, 128), bf16),
        in_specs=[hbm, hbm, hbm, hbm, smem, smem],
        out_specs=vmem,
        scratch_shapes=scratch,
        compiler_params=pltpu.CompilerParams(collective_id=0, has_side_effects=True),
        name="multipole_to_local",
    )(rows, tables, rotation, coaxial, offsets, class_index)
    return jnp.transpose(field, (1, 0, 2))


def solution(mesh):
    placed = (
        P("cell", None, "coef"),
        P(None, "coef", None, None),
        P(None, "coef", None, None),
        P(),
        P(),
    )
    return jax.shard_map(
        on_device, mesh=mesh, in_specs=placed, out_specs=P("cell", None, "coef"), check_vma=False
    )
```

```python
import jax
import jax.numpy as jnp
import numpy as np
from jax import lax
from jax.experimental import pallas as pl
from jax.experimental.pallas import tpu as pltpu
from jax.sharding import PartitionSpec as P

NCLASS = 4
PER = 10
COMPONENTS = 9
CHUNKS = ((0, 4), (4, 9))
ORDER = ("a0", "h0", "a1", "h1", "l0", "l1", "e0", "e1")
MESH = pl.DeviceIdType.MESH


def far_first():
    ways = {}
    for dx in range(4):
        for dy in range(4):
            for dc in range(2):
                if (dx, dy, dc) != (0, 0, 0):
                    ways.setdefault((dx, dy), []).append((dx, dy, dc))
    hops = lambda way: min(way[0], 4 - way[0]) + min(way[1], 4 - way[1])
    keys = sorted(ways, key=lambda way: -hops(way))
    return [ways[key][-1 - turn] for turn in range(2) for key in keys if turn < len(ways[key])]


FAR_FIRST = far_first()
HALF_FAR_FIRST = [
    (dx, dh, dc) for dc in (1, 0) for dx, dh in (
        (2, 1), (2, 0), (1, 1), (3, 1), (0, 1), (1, 0), (3, 0), (0, 0))]


def block_tables():
    degree_list = []
    for block_number in range(8):
        for level in (block_number, 15 - block_number, 16 + block_number, 31 - block_number):
            for order in range(-level, level + 1):
                degree_list.append((level, order))
    order_list = []
    for block_number in range(8):
        if block_number == 0:
            magnitudes = (0, 16, 8, 24)
        else:
            magnitudes = (block_number, 32 - block_number, 16 - block_number, 16 + block_number)
        for size_m in magnitudes:
            for order in [size_m] if size_m == 0 else [size_m, -size_m]:
                for level in range(size_m, 32):
                    order_list.append((level, order))
    where_degree = {pair: index for index, pair in enumerate(degree_list)}
    by_degree = np.zeros((8, 128, 128), np.float32)
    by_order = np.zeros((8, 128, 128), np.float32)
    filled = np.zeros((8, 8), np.int32)
    for order_at, pair in enumerate(order_list):
        degree_at = where_degree[pair]
        a, b = degree_at // 128, order_at // 128
        slot = filled[a, b]
        filled[a, b] += 1
        by_degree[a, b * 16 + slot, degree_at % 128] = 1.0
        by_order[b, (slot // 8) * 64 + a * 8 + slot % 8, order_at % 128] = 1.0
    assert (filled == 16).all()
    levels = np.array([pair[0] for pair in degree_list]).reshape(8, 128)
    orders = np.array([pair[1] for pair in order_list]).reshape(8, 128)
    same_level = (levels[:, :, None] == levels[:, None, :]).astype(np.float32)
    same_order = (orders[:, :, None] == orders[:, None, :]).astype(np.float32)
    return np.stack([by_degree, by_order, same_level, same_order], axis=1)


def tiles(g):
    return CHUNKS[g][1] - CHUNKS[g][0]


def nt(left, right):
    return lax.dot_general(left, right, (((1,), (1,)), ((), ())), preferred_element_type=jnp.float32)


def nn(left, right):
    return jnp.dot(left, right, preferred_element_type=jnp.float32)


def halves_first(rows):
    count, width = rows.shape[0] // 16, rows.shape[1]
    split = rows.reshape(count, 2, 8, width)
    return jnp.concatenate([split[:, h].reshape(count * 8, width) for h in range(2)], axis=0)


def kernel(x_hbm, tables_hbm, rot_hbm, coax_hbm, offs_ref, cls_ref, out_ref, *scratch):
    count = len(CHUNKS)
    names = ("turned", "got", "below", "above", "moved", "back")
    buffers = {name: scratch[i * count:(i + 1) * count] for i, name in enumerate(names)}
    turned, got, below, above, moved, back = (buffers[name] for name in names)
    (x_ref, cells, tables, rot, coax, turning, turning_t, steps, chosen, load_sem, late_sem,
     fwd_send, fwd_recv, halo_send, halo_recv, bwd_send, bwd_recv) = scratch[len(names) * count:]
    cell = lax.axis_index("cell")
    coef = lax.axis_index("coef")
    cell_total = lax.axis_size("cell")
    part = cell % 4
    plane = cell - part
    me = part * 8 + coef
    along, high, low, core = coef % 4, coef // 4, part // 2, part % 2
    up = (cell + 4) % cell_total
    down = (cell + cell_total - 4) % cell_total
    is_first = jnp.logical_and(cell == 0, coef == 0)
    beside_first = jnp.logical_and(coef == 0, jnp.logical_or(up == 0, down == 0))
    knows_first = jnp.logical_and(
        jnp.logical_not(is_first), jnp.logical_or(plane == 0, beside_first))

    xs = [(along + i) % 4 for i in range(4)]
    ys = [(high * 2 + low + i) % 4 for i in range(4)]
    cores = [core, 1 - core]

    def partner(dx, dy, dc):
        to_part = (ys[dy] % 2) * 2 + cores[dc]
        to_coef = (ys[dy] // 2) * 4 + xs[dx]
        return to_part * 8 + to_coef, (plane + to_part, to_coef)

    def half_partner(half, dx, dh, dc):
        to_part = half * 2 + cores[dc]
        to_coef = (high + dh) % 2 * 4 + xs[dx]
        return to_part * 8 + to_coef, (plane + to_part, to_coef)

    barrier = pltpu.get_barrier_semaphore()
    friends = [partner(*step)[1] for step in FAR_FIRST] + [(up, coef), (down, coef)]

    @pl.when(jnp.logical_not(is_first))
    def _():
        for device in friends:
            pl.semaphore_signal(barrier, inc=1, device_id=device, device_id_type=MESH)

    loads = [
        pltpu.make_async_copy(tables_hbm.at[coef], tables, load_sem.at[0]),
        pltpu.make_async_copy(rot_hbm, rot, load_sem.at[1]),
        pltpu.make_async_copy(coax_hbm, coax, load_sem.at[2]),
        pltpu.make_async_copy(x_hbm, x_ref, load_sem.at[3]),
    ]
    for load in (loads[0], loads[1], loads[3], loads[2]):
        load.start()

    @pl.when(is_first)
    def _():
        pl.semaphore_wait(barrier, len(friends))
        for device in friends:
            pl.semaphore_signal(late_sem, inc=1, device_id=device, device_id_type=MESH)

    loads[0].wait()
    loads[1].wait()
    for c in range(NCLASS):
        masked = rot[c, 0] * tables[2]
        turning[c * 128:(c + 1) * 128, :] = nn(tables[0], masked).astype(jnp.bfloat16)

    def send(source, target, send_sem, recv_sem, device):
        pltpu.make_async_remote_copy(
            source, target, send_sem, recv_sem, device_id=device, device_id_type=MESH).start()

    def landed(ref, sem):
        pltpu.make_async_copy(ref, ref, sem).wait()

    def turn(g):
        first, last = CHUNKS[g]
        for at, s0 in enumerate(range(first, last, 2)):
            members = range(s0, min(s0 + 2, last))
            rows = x_ref[s0:members[-1] + 1].reshape(len(members) * 64, 128)
            result = nt(turning[...], rows).reshape(32, 2, 8, len(members) * 64)
            if len(members) == 1:
                result = jnp.concatenate([result[:, 0], result[:, 1]], axis=2)
                turned[g][:, 2 * at] = result.astype(jnp.bfloat16)
            else:
                for h in range(2):
                    turned[g][:, 2 * at + h] = result[:, h].astype(jnp.bfloat16)

    def spread(g):
        for step in FAR_FIRST:
            other, device = partner(*step)

            @pl.when(jnp.logical_or(plane != 0, other != 0))
            def _():
                send(turned[g].at[other], got[g].at[me], fwd_send.at[g], fwd_recv.at[g], device)

        pltpu.make_async_copy(turned[g].at[me], got[g].at[me], fwd_recv.at[g]).start()

    def greet_first():
        @pl.when(knows_first)
        def _():
            pl.semaphore_wait(late_sem, 1)

        @pl.when(jnp.logical_and(knows_first, plane == 0))
        def _():
            for g in range(count):
                send(turned[g].at[0], got[g].at[me], fwd_send.at[g], fwd_recv.at[g], (0, 0))

    def pick(k, carry):
        seen, kept = carry[0], carry[1:]
        hit = cls_ref[k] == part
        kept = tuple(
            jnp.where(jnp.logical_and(hit, seen == p), k, old) for p, old in enumerate(kept))
        return (seen + jnp.where(hit, 1, 0),) + kept

    def prepare_steps():
        picked = lax.fori_loop(0, NCLASS * PER, pick, (jnp.int32(0),) * (PER + 1))[1:]
        for p in range(PER):
            chosen[p] = picked[p]
        loads[2].wait()

        def prepare(p, carry):
            masked = coax[chosen[p], 0] * tables[3]
            half = nn(tables[1], masked).astype(jnp.bfloat16)
            steps[p] = nt(half, tables[1]).astype(jnp.bfloat16)
            return carry

        lax.fori_loop(0, PER, prepare, 0)

    def prepare_return():
        rows = halves_first(turning[...].astype(jnp.float32))
        for c in range(NCLASS):
            turning_t[:, c * 128:(c + 1) * 128] = rows[c * 128:(c + 1) * 128].T.astype(jnp.bfloat16)

    def lay(buffer, row, groups, g):
        first, last = CHUNKS[g]
        for j in range(groups):
            for at, s0 in enumerate(range(first, last, 2)):
                if s0 + 1 == last:
                    block = buffer[j * 8:(j + 1) * 8, 2 * at].astype(jnp.float32).reshape(64, 128).T
                    cells[s0, row + j * 64:row + j * 64 + 64, :] = jnp.concatenate(
                        [block[:64], block[64:]], axis=1)
                    continue
                block = jnp.concatenate(
                    [buffer[j * 8:(j + 1) * 8, 2 * at + h].astype(jnp.float32).reshape(64, 128)
                     for h in range(2)], axis=0).T
                for m in range(2):
                    cells[s0 + m, row + j * 64:row + j * 64 + 64, :] = block[m * 64:(m + 1) * 64]

    def arrive(g):
        landed(got[g], fwd_recv.at[g])
        send(got[g].at[pl.ds(0, 16)], above[g], halo_send.at[g, 1], halo_recv.at[g, 1], (down, coef))
        send(got[g].at[pl.ds(16, 16)], below[g], halo_send.at[g, 0], halo_recv.at[g, 0], (up, coef))
        lay(got[g], 128, 4, g)

    def translate(g, half):
        first, last = CHUNKS[g]
        if half:
            landed(above[g], halo_recv.at[g, 1])
            lay(above[g], 384, 2, g)
        else:
            landed(below[g], halo_recv.at[g, 0])
            lay(below[g], 0, 2, g)
        matrices = jnp.concatenate([steps[p] for p in range(PER)], axis=1)
        starts = [128 + half * 128 + offs_ref[chosen[p]] for p in range(PER)]
        for at, s0 in enumerate(range(first, last, 2)):
            members = range(s0, min(s0 + 2, last))
            width = 64 * len(members)
            pieces = []
            for p in range(PER):
                pieces.append(jnp.concatenate(
                    [cells[s, pl.ds(starts[p] + i * 64, 64), :] for i in range(2) for s in members],
                    axis=0).astype(jnp.bfloat16))
            result = nt(matrices, jnp.concatenate(pieces, axis=1))
            for i in range(2):
                row = (half * 2 + i) * 8
                piece = result[:, i * width:(i + 1) * width]
                if len(members) == 1:
                    piece = jnp.concatenate([piece[:64], piece[64:]], axis=1)
                    moved[g][row:row + 8, 2 * at] = piece.reshape(8, 8, 128).astype(jnp.bfloat16)
                else:
                    for h in range(2):
                        moved[g][row:row + 8, 2 * at + h] = (
                            piece[h * 64:(h + 1) * 64].reshape(8, 8, 128).astype(jnp.bfloat16))
        for step in HALF_FAR_FIRST:
            other, device = half_partner(half, *step)
            if step == (0, 0, 0):
                @pl.when(low != half)
                def _():
                    send(moved[g].at[other], back[g].at[me], bwd_send.at[g, half], bwd_recv.at[g], device)

                @pl.when(low == half)
                def _():
                    pltpu.make_async_copy(moved[g].at[me], back[g].at[me], bwd_recv.at[g]).start()
            else:
                send(moved[g].at[other], back[g].at[me], bwd_send.at[g, half], bwd_recv.at[g], device)

    def finish(g):
        first, last = CHUNKS[g]
        landed(back[g], bwd_recv.at[g])
        matrix = turning_t[...]
        for at, s0 in enumerate(range(first, last, 2)):
            if s0 + 1 == last:
                block = back[g][:, 2 * at].reshape(256, 128)
                block = jnp.concatenate([block[:, :64], block[:, 64:]], axis=0)
                out_ref[s0] = nn(matrix, block).T.astype(jnp.bfloat16)
                continue
            block = jnp.concatenate([back[g][:, 2 * at + h].reshape(256, 128) for h in range(2)], axis=0)
            piece = nn(matrix, block).T.astype(jnp.bfloat16)
            for m in range(2):
                out_ref[s0 + m] = piece[m * 64:(m + 1) * 64]

    loads[3].wait()
    for g in range(count):
        turn(g)
        if g == 0:
            @pl.when(jnp.logical_not(is_first))
            def _():
                pl.semaphore_wait(barrier, len(friends) - jnp.where(knows_first, 1, 0))
        spread(g)
    prepare_steps()
    prepare_return()
    greet_first()
    stages = {
        "a": arrive, "h": lambda g: translate(g, 1), "l": lambda g: translate(g, 0), "e": finish,
    }
    for token in ORDER:
        stages[token[0]](int(token[1:]))

    for g in range(count):
        landed(turned[g].at[pl.ds(0, 31)], fwd_send.at[g])
        landed(below[g], halo_send.at[g, 0])
        landed(above[g], halo_send.at[g, 1])
        for half in range(2):
            @pl.when(low == half)
            def _():
                landed(moved[g].at[pl.ds(0, 15)], bwd_send.at[g, half])

            @pl.when(low != half)
            def _():
                landed(moved[g].at[pl.ds(0, 16)], bwd_send.at[g, half])


def on_device(multipoles, rotation, coaxial, offsets, class_index):
    tables = jnp.asarray(block_tables(), jnp.bfloat16)
    rows = jnp.transpose(multipoles, (1, 0, 2))
    vmem = pl.BlockSpec(memory_space=pltpu.VMEM)
    smem = pl.BlockSpec(memory_space=pltpu.SMEM)
    hbm = pl.BlockSpec(memory_space=pl.ANY)
    count = len(CHUNKS)
    bf16 = jnp.bfloat16
    scratch = []
    for outer in (32, 32, 16, 16, 32, 32):
        scratch += [pltpu.VMEM((outer, tiles(g), 8, 128), bf16) for g in range(count)]
    dma = pltpu.SemaphoreType.DMA
    scratch += [
        pltpu.VMEM((COMPONENTS, 64, 128), bf16),
        pltpu.VMEM((COMPONENTS, 512, 128), jnp.float32),
        pltpu.VMEM((4, 128, 128), bf16),
        pltpu.VMEM((NCLASS, 1, 128, 128), bf16),
        pltpu.VMEM((NCLASS * PER, 1, 128, 128), bf16),
        pltpu.VMEM((NCLASS * 128, 128), bf16),
        pltpu.VMEM((128, NCLASS * 128), bf16),
        pltpu.VMEM((PER, 128, 128), bf16),
        pltpu.SMEM((PER,), jnp.int32),
        dma((4,)), pltpu.SemaphoreType.REGULAR,
        dma((count,)), dma((count,)),
        dma((count, 2)), dma((count, 2)),
        dma((count, 2)), dma((count,)),
    ]
    field = pl.pallas_call(
        kernel,
        out_shape=jax.ShapeDtypeStruct((COMPONENTS, 64, 128), bf16),
        in_specs=[hbm, hbm, hbm, hbm, smem, smem],
        out_specs=vmem,
        scratch_shapes=scratch,
        compiler_params=pltpu.CompilerParams(collective_id=0, has_side_effects=True),
        name="multipole_to_local",
    )(rows, tables, rotation, coaxial, offsets, class_index)
    return jnp.transpose(field, (1, 0, 2))


def solution(mesh):
    placed = (
        P("cell", None, "coef"),
        P(None, "coef", None, None),
        P(None, "coef", None, None),
        P(),
        P(),
    )
    return jax.shard_map(
        on_device, mesh=mesh, in_specs=placed, out_specs=P("cell", None, "coef"), check_vma=False
    )
```

```python
import jax
import jax.numpy as jnp
import numpy as np
from jax import lax
from jax.experimental import pallas as pl
from jax.experimental.pallas import tpu as pltpu
from jax.sharding import PartitionSpec as P

NCLASS = 4
PER = 10
COMPONENTS = 9
CHUNKS = ((0, 4), (4, 9))
ORDER = ("b0", "a0", "y0", "b1", "a1", "h0", "y1", "l0", "h1", "l1", "e0", "e1")
MESH = pl.DeviceIdType.MESH


def far_first():
    ways = {}
    for dx in range(4):
        for dy in range(4):
            for dc in range(2):
                if (dx, dy, dc) != (0, 0, 0):
                    ways.setdefault((dx, dy), []).append((dx, dy, dc))
    hops = lambda way: min(way[0], 4 - way[0]) + min(way[1], 4 - way[1])
    keys = sorted(ways, key=lambda way: -hops(way))
    return [ways[key][-1 - turn] for turn in range(2) for key in keys if turn < len(ways[key])]


FAR_FIRST = far_first()
HALF_FAR_FIRST = [
    (dx, dh, dc) for dc in (1, 0) for dx, dh in (
        (2, 1), (2, 0), (1, 1), (3, 1), (0, 1), (1, 0), (3, 0), (0, 0))]


def block_tables():
    degree_list = []
    for block_number in range(8):
        for level in (block_number, 15 - block_number, 16 + block_number, 31 - block_number):
            for order in range(-level, level + 1):
                degree_list.append((level, order))
    order_list = []
    for block_number in range(8):
        if block_number == 0:
            magnitudes = (0, 16, 8, 24)
        else:
            magnitudes = (block_number, 32 - block_number, 16 - block_number, 16 + block_number)
        for size_m in magnitudes:
            for order in [size_m] if size_m == 0 else [size_m, -size_m]:
                for level in range(size_m, 32):
                    order_list.append((level, order))
    where_degree = {pair: index for index, pair in enumerate(degree_list)}
    by_degree = np.zeros((8, 128, 128), np.float32)
    by_order = np.zeros((8, 128, 128), np.float32)
    filled = np.zeros((8, 8), np.int32)
    for order_at, pair in enumerate(order_list):
        degree_at = where_degree[pair]
        a, b = degree_at // 128, order_at // 128
        slot = filled[a, b]
        filled[a, b] += 1
        by_degree[a, b * 16 + slot, degree_at % 128] = 1.0
        by_order[b, (slot // 8) * 64 + a * 8 + slot % 8, order_at % 128] = 1.0
    assert (filled == 16).all()
    levels = np.array([pair[0] for pair in degree_list]).reshape(8, 128)
    orders = np.array([pair[1] for pair in order_list]).reshape(8, 128)
    same_level = (levels[:, :, None] == levels[:, None, :]).astype(np.float32)
    same_order = (orders[:, :, None] == orders[:, None, :]).astype(np.float32)
    return np.stack([by_degree, by_order, same_level, same_order], axis=1)


def tiles(g):
    return CHUNKS[g][1] - CHUNKS[g][0]


def nt(left, right):
    return lax.dot_general(left, right, (((1,), (1,)), ((), ())), preferred_element_type=jnp.float32)


def nn(left, right):
    return jnp.dot(left, right, preferred_element_type=jnp.float32)


def halves_first(rows):
    count, width = rows.shape[0] // 16, rows.shape[1]
    split = rows.reshape(count, 2, 8, width)
    return jnp.concatenate([split[:, h].reshape(count * 8, width) for h in range(2)], axis=0)


def kernel(x_hbm, tables_hbm, rot_hbm, coax_hbm, offs_ref, cls_ref, out_hbm, *scratch):
    count = len(CHUNKS)
    names = ("turned", "got", "below", "above", "moved", "back")
    buffers = {name: scratch[i * count:(i + 1) * count] for i, name in enumerate(names)}
    turned, got, below, above, moved, back = (buffers[name] for name in names)
    (x_ref, out_ref, cells, tables, rot, coax, turning, turning_t, steps, chosen, load_sem, out_sem, late_sem,
     fwd_send, fwd_recv, halo_send, halo_recv, bwd_send, bwd_recv) = scratch[len(names) * count:]
    cell = lax.axis_index("cell")
    coef = lax.axis_index("coef")
    cell_total = lax.axis_size("cell")
    part = cell % 4
    plane = cell - part
    me = part * 8 + coef
    along, high, low, core = coef % 4, coef // 4, part // 2, part % 2
    up = (cell + 4) % cell_total
    down = (cell + cell_total - 4) % cell_total
    is_first = jnp.logical_and(cell == 0, coef == 0)
    beside_first = jnp.logical_and(coef == 0, jnp.logical_or(up == 0, down == 0))
    knows_first = jnp.logical_and(
        jnp.logical_not(is_first), jnp.logical_or(plane == 0, beside_first))

    xs = [(along + i) % 4 for i in range(4)]
    ys = [(high * 2 + low + i) % 4 for i in range(4)]
    cores = [core, 1 - core]

    def partner(dx, dy, dc):
        to_part = (ys[dy] % 2) * 2 + cores[dc]
        to_coef = (ys[dy] // 2) * 4 + xs[dx]
        return to_part * 8 + to_coef, (plane + to_part, to_coef)

    def half_partner(half, dx, dh, dc):
        to_part = half * 2 + cores[dc]
        to_coef = (high + dh) % 2 * 4 + xs[dx]
        return to_part * 8 + to_coef, (plane + to_part, to_coef)

    barrier = pltpu.get_barrier_semaphore()
    friends = [partner(*step)[1] for step in FAR_FIRST] + [(up, coef), (down, coef)]

    @pl.when(jnp.logical_not(is_first))
    def _():
        for device in friends:
            pl.semaphore_signal(barrier, inc=1, device_id=device, device_id_type=MESH)

    loads = [
        pltpu.make_async_copy(tables_hbm.at[coef], tables, load_sem.at[0]),
        pltpu.make_async_copy(rot_hbm, rot, load_sem.at[1]),
        pltpu.make_async_copy(coax_hbm, coax, load_sem.at[2]),
        pltpu.make_async_copy(x_hbm, x_ref, load_sem.at[3]),
    ]
    for load in (loads[0], loads[1], loads[3], loads[2]):
        load.start()

    @pl.when(is_first)
    def _():
        pl.semaphore_wait(barrier, len(friends))
        for device in friends:
            pl.semaphore_signal(late_sem, inc=1, device_id=device, device_id_type=MESH)

    loads[0].wait()
    loads[1].wait()
    for c in range(NCLASS):
        masked = rot[c, 0] * tables[2]
        turning[c * 128:(c + 1) * 128, :] = nn(tables[0], masked).astype(jnp.bfloat16)

    def send(source, target, send_sem, recv_sem, device):
        pltpu.make_async_remote_copy(
            source, target, send_sem, recv_sem, device_id=device, device_id_type=MESH).start()

    def landed(ref, sem):
        pltpu.make_async_copy(ref, ref, sem).wait()

    def turn(g):
        first, last = CHUNKS[g]
        for at, s0 in enumerate(range(first, last, 2)):
            members = range(s0, min(s0 + 2, last))
            rows = x_ref[s0:members[-1] + 1].reshape(len(members) * 64, 128)
            result = nt(turning[...], rows).reshape(32, 2, 8, len(members) * 64)
            if len(members) == 1:
                result = jnp.concatenate([result[:, 0], result[:, 1]], axis=2)
                turned[g][:, 2 * at] = result.astype(jnp.bfloat16)
            else:
                for h in range(2):
                    turned[g][:, 2 * at + h] = result[:, h].astype(jnp.bfloat16)

    def spread(g):
        for step in FAR_FIRST:
            other, device = partner(*step)

            @pl.when(jnp.logical_or(plane != 0, other != 0))
            def _():
                send(turned[g].at[other], got[g].at[me], fwd_send.at[g], fwd_recv.at[g, low], device)

        pltpu.make_async_copy(turned[g].at[me], got[g].at[me], fwd_recv.at[g, low]).start()

    def greet_first():
        @pl.when(knows_first)
        def _():
            pl.semaphore_wait(late_sem, 1)

        @pl.when(jnp.logical_and(knows_first, plane == 0))
        def _():
            for g in range(count):
                send(turned[g].at[0], got[g].at[me], fwd_send.at[g], fwd_recv.at[g, low], (0, 0))

    def pick(k, carry):
        seen, kept = carry[0], carry[1:]
        hit = cls_ref[k] == part
        kept = tuple(
            jnp.where(jnp.logical_and(hit, seen == p), k, old) for p, old in enumerate(kept))
        return (seen + jnp.where(hit, 1, 0),) + kept

    def prepare_steps():
        picked = lax.fori_loop(0, NCLASS * PER, pick, (jnp.int32(0),) * (PER + 1))[1:]
        for p in range(PER):
            chosen[p] = picked[p]
        loads[2].wait()

        def prepare(p, carry):
            masked = coax[chosen[p], 0] * tables[3]
            half = nn(tables[1], masked).astype(jnp.bfloat16)
            steps[p] = nt(half, tables[1]).astype(jnp.bfloat16)
            return carry

        lax.fori_loop(0, PER, prepare, 0)

    def prepare_return():
        rows = halves_first(turning[...].astype(jnp.float32))
        for c in range(NCLASS):
            turning_t[:, c * 128:(c + 1) * 128] = rows[c * 128:(c + 1) * 128].T.astype(jnp.bfloat16)

    def lay(buffer, row, groups, g):
        first, last = CHUNKS[g]
        for j in range(groups):
            for at, s0 in enumerate(range(first, last, 2)):
                if s0 + 1 == last:
                    block = buffer[j * 8:(j + 1) * 8, 2 * at].astype(jnp.float32).reshape(64, 128).T
                    cells[s0, row + j * 64:row + j * 64 + 64, :] = jnp.concatenate(
                        [block[:64], block[64:]], axis=1)
                    continue
                block = jnp.concatenate(
                    [buffer[j * 8:(j + 1) * 8, 2 * at + h].astype(jnp.float32).reshape(64, 128)
                     for h in range(2)], axis=0).T
                for m in range(2):
                    cells[s0 + m, row + j * 64:row + j * 64 + 64, :] = block[m * 64:(m + 1) * 64]

    def rise(g):
        upper = got[g].at[pl.ds(16, 16)]
        landed(upper, fwd_recv.at[g, 1])
        send(upper, below[g], halo_send.at[g, 0], halo_recv.at[g, 0], (up, coef))

    def sink(g):
        lower = got[g].at[pl.ds(0, 16)]
        landed(lower, fwd_recv.at[g, 0])
        send(lower, above[g], halo_send.at[g, 1], halo_recv.at[g, 1], (down, coef))

    def translate(g, half):
        first, last = CHUNKS[g]
        if half:
            landed(above[g], halo_recv.at[g, 1])
            lay(above[g], 384, 2, g)
        else:
            landed(below[g], halo_recv.at[g, 0])
            lay(below[g], 0, 2, g)
        matrices = jnp.concatenate([steps[p] for p in range(PER)], axis=1)
        starts = [128 + half * 128 + offs_ref[chosen[p]] for p in range(PER)]
        for at, s0 in enumerate(range(first, last, 2)):
            members = range(s0, min(s0 + 2, last))
            width = 64 * len(members)
            pieces = []
            for p in range(PER):
                pieces.append(jnp.concatenate(
                    [cells[s, pl.ds(starts[p] + i * 64, 64), :] for i in range(2) for s in members],
                    axis=0).astype(jnp.bfloat16))
            result = nt(matrices, jnp.concatenate(pieces, axis=1))
            for i in range(2):
                row = (half * 2 + i) * 8
                piece = result[:, i * width:(i + 1) * width]
                if len(members) == 1:
                    piece = jnp.concatenate([piece[:64], piece[64:]], axis=1)
                    moved[g][row:row + 8, 2 * at] = piece.reshape(8, 8, 128).astype(jnp.bfloat16)
                else:
                    for h in range(2):
                        moved[g][row:row + 8, 2 * at + h] = (
                            piece[h * 64:(h + 1) * 64].reshape(8, 8, 128).astype(jnp.bfloat16))
        for step in HALF_FAR_FIRST:
            other, device = half_partner(half, *step)
            if step == (0, 0, 0):
                @pl.when(low != half)
                def _():
                    send(moved[g].at[other], back[g].at[me], bwd_send.at[g, half], bwd_recv.at[g], device)

                @pl.when(low == half)
                def _():
                    pltpu.make_async_copy(moved[g].at[me], back[g].at[me], bwd_recv.at[g]).start()
            else:
                send(moved[g].at[other], back[g].at[me], bwd_send.at[g, half], bwd_recv.at[g], device)

    def finish(g):
        first, last = CHUNKS[g]
        landed(back[g], bwd_recv.at[g])
        matrix = turning_t[...]
        for at, s0 in enumerate(range(first, last, 2)):
            if s0 + 1 == last:
                block = back[g][:, 2 * at].reshape(256, 128)
                block = jnp.concatenate([block[:, :64], block[:, 64:]], axis=0)
                out_ref[s0] = nn(matrix, block).T.astype(jnp.bfloat16)
                continue
            block = jnp.concatenate([back[g][:, 2 * at + h].reshape(256, 128) for h in range(2)], axis=0)
            piece = nn(matrix, block).T.astype(jnp.bfloat16)
            for m in range(2):
                out_ref[s0 + m] = piece[m * 64:(m + 1) * 64]
        pltpu.make_async_copy(out_ref.at[first:last], out_hbm.at[first:last], out_sem.at[g]).start()

    loads[3].wait()
    for g in range(count):
        turn(g)
        if g == 0:
            @pl.when(jnp.logical_not(is_first))
            def _():
                pl.semaphore_wait(barrier, len(friends) - jnp.where(knows_first, 1, 0))
        spread(g)

    prepare_steps()
    prepare_return()
    greet_first()
    stages = {
        "b": rise, "a": sink, "y": lambda g: lay(got[g], 128, 4, g), "h": lambda g: translate(g, 1), "l": lambda g: translate(g, 0), "e": finish,
    }
    for token in ORDER:
        stages[token[0]](int(token[1:]))

    for g in range(count):
        landed(turned[g].at[pl.ds(0, 31)], fwd_send.at[g])
        landed(below[g], halo_send.at[g, 0])
        landed(above[g], halo_send.at[g, 1])
        for half in range(2):
            @pl.when(low == half)
            def _():
                landed(moved[g].at[pl.ds(0, 15)], bwd_send.at[g, half])

            @pl.when(low != half)
            def _():
                landed(moved[g].at[pl.ds(0, 16)], bwd_send.at[g, half])

    for g, (first, last) in enumerate(CHUNKS):
        landed(out_ref.at[first:last], out_sem.at[g])


def on_device(multipoles, rotation, coaxial, offsets, class_index):
    tables = jnp.asarray(block_tables(), jnp.bfloat16)
    rows = jnp.transpose(multipoles, (1, 0, 2))
    smem = pl.BlockSpec(memory_space=pltpu.SMEM)
    hbm = pl.BlockSpec(memory_space=pl.ANY)
    count = len(CHUNKS)
    bf16 = jnp.bfloat16
    scratch = []
    for outer in (32, 32, 16, 16, 32, 32):
        scratch += [pltpu.VMEM((outer, tiles(g), 8, 128), bf16) for g in range(count)]
    dma = pltpu.SemaphoreType.DMA
    scratch += [
        pltpu.VMEM((COMPONENTS, 64, 128), bf16),
        pltpu.VMEM((COMPONENTS, 64, 128), bf16),
        pltpu.VMEM((COMPONENTS, 512, 128), jnp.float32),
        pltpu.VMEM((4, 128, 128), bf16),
        pltpu.VMEM((NCLASS, 1, 128, 128), bf16),
        pltpu.VMEM((NCLASS * PER, 1, 128, 128), bf16),
        pltpu.VMEM((NCLASS * 128, 128), bf16),
        pltpu.VMEM((128, NCLASS * 128), bf16),
        pltpu.VMEM((PER, 128, 128), bf16),
        pltpu.SMEM((PER,), jnp.int32),
        dma((4,)), dma((count,)), pltpu.SemaphoreType.REGULAR,
        dma((count,)), dma((count, 2)),
        dma((count, 2)), dma((count, 2)),
        dma((count, 2)), dma((count,)),
    ]
    field = pl.pallas_call(
        kernel,
        out_shape=jax.ShapeDtypeStruct((COMPONENTS, 64, 128), bf16),
        in_specs=[hbm, hbm, hbm, hbm, smem, smem],
        out_specs=hbm,
        scratch_shapes=scratch,
        compiler_params=pltpu.CompilerParams(collective_id=0, has_side_effects=True),
        name="multipole_to_local",
    )(rows, tables, rotation, coaxial, offsets, class_index)
    return jnp.transpose(field, (1, 0, 2))


def solution(mesh):
    placed = (
        P("cell", None, "coef"),
        P(None, "coef", None, None),
        P(None, "coef", None, None),
        P(),
        P(),
    )
    return jax.shard_map(
        on_device, mesh=mesh, in_specs=placed, out_specs=P("cell", None, "coef"), check_vma=False
    )
```

```python
import jax
import jax.numpy as jnp
import numpy as np
from jax import lax
from jax.experimental import pallas as pl
from jax.experimental.pallas import tpu as pltpu
from jax.sharding import PartitionSpec as P

NCLASS = 4
PER = 10
COMPONENTS = 9
CHUNKS = ((0, 2), (2, 6), (6, 9))
ORDER = (
    "b0", "a0", "y0", "b1", "a1", "y1", "h0", "b2", "a2", "l0",
    "h1", "y2", "l1", "h2", "l2", "e0", "e1", "e2",
)
MESH = pl.DeviceIdType.MESH


def far_first():
    ways = {}
    for dx in range(4):
        for dy in range(4):
            for dc in range(2):
                if (dx, dy, dc) != (0, 0, 0):
                    ways.setdefault((dx, dy), []).append((dx, dy, dc))
    hops = lambda way: min(way[0], 4 - way[0]) + min(way[1], 4 - way[1])
    keys = sorted(ways, key=lambda way: -hops(way))
    return [ways[key][-1 - turn] for turn in range(2) for key in keys if turn < len(ways[key])]


FAR_FIRST = far_first()
HALF_FAR_FIRST = [
    (dx, dh, dc) for dc in (1, 0) for dx, dh in (
        (2, 1), (2, 0), (1, 1), (3, 1), (0, 1), (1, 0), (3, 0), (0, 0))]


def block_tables():
    degree_list = []
    for block_number in range(8):
        for level in (block_number, 15 - block_number, 16 + block_number, 31 - block_number):
            for order in range(-level, level + 1):
                degree_list.append((level, order))
    order_list = []
    for block_number in range(8):
        if block_number == 0:
            magnitudes = (0, 16, 8, 24)
        else:
            magnitudes = (block_number, 32 - block_number, 16 - block_number, 16 + block_number)
        for size_m in magnitudes:
            for order in [size_m] if size_m == 0 else [size_m, -size_m]:
                for level in range(size_m, 32):
                    order_list.append((level, order))
    where_degree = {pair: index for index, pair in enumerate(degree_list)}
    by_degree = np.zeros((8, 128, 128), np.float32)
    by_order = np.zeros((8, 128, 128), np.float32)
    filled = np.zeros((8, 8), np.int32)
    for order_at, pair in enumerate(order_list):
        degree_at = where_degree[pair]
        a, b = degree_at // 128, order_at // 128
        slot = filled[a, b]
        filled[a, b] += 1
        by_degree[a, b * 16 + slot, degree_at % 128] = 1.0
        by_order[b, (slot // 8) * 64 + a * 8 + slot % 8, order_at % 128] = 1.0
    assert (filled == 16).all()
    levels = np.array([pair[0] for pair in degree_list]).reshape(8, 128)
    orders = np.array([pair[1] for pair in order_list]).reshape(8, 128)
    same_level = (levels[:, :, None] == levels[:, None, :]).astype(np.float32)
    same_order = (orders[:, :, None] == orders[:, None, :]).astype(np.float32)
    return np.stack([by_degree, by_order, same_level, same_order], axis=1)


def tiles(g):
    return CHUNKS[g][1] - CHUNKS[g][0]


def nt(left, right):
    return lax.dot_general(left, right, (((1,), (1,)), ((), ())), preferred_element_type=jnp.float32)


def nn(left, right):
    return jnp.dot(left, right, preferred_element_type=jnp.float32)


def halves_first(rows):
    count, width = rows.shape[0] // 16, rows.shape[1]
    split = rows.reshape(count, 2, 8, width)
    return jnp.concatenate([split[:, h].reshape(count * 8, width) for h in range(2)], axis=0)


def kernel(x_hbm, tables_hbm, rot_hbm, coax_hbm, offs_hbm, cls_hbm, out_hbm, *scratch):
    count = len(CHUNKS)
    names = ("turned", "got", "below", "above", "moved", "back")
    buffers = {name: scratch[i * count:(i + 1) * count] for i, name in enumerate(names)}
    turned, got, below, above, moved, back = (buffers[name] for name in names)
    (offs_ref, cls_ref, x_ref, out_ref, cells, tables, rot, coax, turning, turning_t, steps, chosen, load_sem, out_sem, late_sem,
     fwd_send, fwd_recv, halo_send, halo_recv, bwd_send, bwd_recv) = scratch[len(names) * count:]
    cell = lax.axis_index("cell")
    coef = lax.axis_index("coef")
    cell_total = lax.axis_size("cell")
    part = cell % 4
    plane = cell - part
    me = part * 8 + coef
    along, high, low, core = coef % 4, coef // 4, part // 2, part % 2
    up = (cell + 4) % cell_total
    down = (cell + cell_total - 4) % cell_total
    is_first = jnp.logical_and(cell == 0, coef == 0)
    beside_first = jnp.logical_and(coef == 0, jnp.logical_or(up == 0, down == 0))
    knows_first = jnp.logical_and(
        jnp.logical_not(is_first), jnp.logical_or(plane == 0, beside_first))

    xs = [(along + i) % 4 for i in range(4)]
    ys = [(high * 2 + low + i) % 4 for i in range(4)]
    cores = [core, 1 - core]

    def partner(dx, dy, dc):
        to_part = (ys[dy] % 2) * 2 + cores[dc]
        to_coef = (ys[dy] // 2) * 4 + xs[dx]
        return to_part * 8 + to_coef, (plane + to_part, to_coef)

    def half_partner(half, dx, dh, dc):
        to_part = half * 2 + cores[dc]
        to_coef = (high + dh) % 2 * 4 + xs[dx]
        return to_part * 8 + to_coef, (plane + to_part, to_coef)

    barrier = pltpu.get_barrier_semaphore()
    friends = [partner(*step)[1] for step in FAR_FIRST] + [(up, coef), (down, coef)]

    @pl.when(jnp.logical_not(is_first))
    def _():
        for device in friends:
            pl.semaphore_signal(barrier, inc=1, device_id=device, device_id_type=MESH)

    loads = [
        pltpu.make_async_copy(tables_hbm.at[coef], tables, load_sem.at[0]),
        pltpu.make_async_copy(rot_hbm, rot, load_sem.at[1]),
        pltpu.make_async_copy(coax_hbm, coax, load_sem.at[2]),
        pltpu.make_async_copy(x_hbm, x_ref, load_sem.at[3]),
        pltpu.make_async_copy(offs_hbm, offs_ref, load_sem.at[4]),
        pltpu.make_async_copy(cls_hbm, cls_ref, load_sem.at[5]),
    ]
    for load in (loads[0], loads[1], loads[3], loads[2], loads[4], loads[5]):
        load.start()

    @pl.when(is_first)
    def _():
        pl.semaphore_wait(barrier, len(friends))
        for device in friends:
            pl.semaphore_signal(late_sem, inc=1, device_id=device, device_id_type=MESH)

    loads[0].wait()
    loads[1].wait()
    for c in range(NCLASS):
        masked = rot[c, 0] * tables[2]
        turning[c * 128:(c + 1) * 128, :] = nn(tables[0], masked).astype(jnp.bfloat16)

    def send(source, target, send_sem, recv_sem, device):
        pltpu.make_async_remote_copy(
            source, target, send_sem, recv_sem, device_id=device, device_id_type=MESH).start()

    def landed(ref, sem):
        pltpu.make_async_copy(ref, ref, sem).wait()

    def turn(g):
        first, last = CHUNKS[g]
        for at, s0 in enumerate(range(first, last, 2)):
            members = range(s0, min(s0 + 2, last))
            rows = x_ref[s0:members[-1] + 1].reshape(len(members) * 64, 128)
            result = nt(turning[...], rows).reshape(32, 2, 8, len(members) * 64)
            if len(members) == 1:
                result = jnp.concatenate([result[:, 0], result[:, 1]], axis=2)
                turned[g][:, 2 * at] = result.astype(jnp.bfloat16)
            else:
                for h in range(2):
                    turned[g][:, 2 * at + h] = result[:, h].astype(jnp.bfloat16)

    def spread(g):
        for step in FAR_FIRST:
            other, device = partner(*step)

            @pl.when(jnp.logical_or(plane != 0, other != 0))
            def _():
                send(turned[g].at[other], got[g].at[me], fwd_send.at[g], fwd_recv.at[g, low], device)

        pltpu.make_async_copy(turned[g].at[me], got[g].at[me], fwd_recv.at[g, low]).start()

    def greet_first():
        @pl.when(knows_first)
        def _():
            pl.semaphore_wait(late_sem, 1)

        @pl.when(jnp.logical_and(knows_first, plane == 0))
        def _():
            for g in range(count):
                send(turned[g].at[0], got[g].at[me], fwd_send.at[g], fwd_recv.at[g, low], (0, 0))

    def pick(k, carry):
        seen, kept = carry[0], carry[1:]
        hit = cls_ref[k] == part
        kept = tuple(
            jnp.where(jnp.logical_and(hit, seen == p), k, old) for p, old in enumerate(kept))
        return (seen + jnp.where(hit, 1, 0),) + kept

    def prepare_steps():
        loads[4].wait()
        loads[5].wait()
        picked = lax.fori_loop(0, NCLASS * PER, pick, (jnp.int32(0),) * (PER + 1))[1:]
        for p in range(PER):
            chosen[p] = picked[p]
        loads[2].wait()

        def prepare(p, carry):
            masked = coax[chosen[p], 0] * tables[3]
            half = nn(tables[1], masked).astype(jnp.bfloat16)
            steps[p] = nt(half, tables[1]).astype(jnp.bfloat16)
            return carry

        lax.fori_loop(0, PER, prepare, 0)

    def prepare_return():
        rows = halves_first(turning[...].astype(jnp.float32))
        for c in range(NCLASS):
            turning_t[:, c * 128:(c + 1) * 128] = rows[c * 128:(c + 1) * 128].T.astype(jnp.bfloat16)

    def lay(buffer, row, groups, g):
        first, last = CHUNKS[g]
        for j in range(groups):
            for at, s0 in enumerate(range(first, last, 2)):
                if s0 + 1 == last:
                    block = buffer[j * 8:(j + 1) * 8, 2 * at].astype(jnp.float32).reshape(64, 128).T
                    cells[s0, row + j * 64:row + j * 64 + 64, :] = jnp.concatenate(
                        [block[:64], block[64:]], axis=1)
                    continue
                block = jnp.concatenate(
                    [buffer[j * 8:(j + 1) * 8, 2 * at + h].astype(jnp.float32).reshape(64, 128)
                     for h in range(2)], axis=0).T
                for m in range(2):
                    cells[s0 + m, row + j * 64:row + j * 64 + 64, :] = block[m * 64:(m + 1) * 64]

    def rise(g):
        upper = got[g].at[pl.ds(16, 16)]
        landed(upper, fwd_recv.at[g, 1])
        send(upper, below[g], halo_send.at[g, 0], halo_recv.at[g, 0], (up, coef))

    def sink(g):
        lower = got[g].at[pl.ds(0, 16)]
        landed(lower, fwd_recv.at[g, 0])
        send(lower, above[g], halo_send.at[g, 1], halo_recv.at[g, 1], (down, coef))

    def translate(g, half):
        first, last = CHUNKS[g]
        if half:
            landed(above[g], halo_recv.at[g, 1])
            lay(above[g], 384, 2, g)
        else:
            landed(below[g], halo_recv.at[g, 0])
            lay(below[g], 0, 2, g)
        matrices = jnp.concatenate([steps[p] for p in range(PER)], axis=1)
        starts = [128 + half * 128 + offs_ref[chosen[p]] for p in range(PER)]
        for at, s0 in enumerate(range(first, last, 2)):
            members = range(s0, min(s0 + 2, last))
            width = 64 * len(members)
            pieces = []
            for p in range(PER):
                pieces.append(jnp.concatenate(
                    [cells[s, pl.ds(starts[p] + i * 64, 64), :] for i in range(2) for s in members],
                    axis=0).astype(jnp.bfloat16))
            result = nt(matrices, jnp.concatenate(pieces, axis=1))
            for i in range(2):
                row = (half * 2 + i) * 8
                piece = result[:, i * width:(i + 1) * width]
                if len(members) == 1:
                    piece = jnp.concatenate([piece[:64], piece[64:]], axis=1)
                    moved[g][row:row + 8, 2 * at] = piece.reshape(8, 8, 128).astype(jnp.bfloat16)
                else:
                    for h in range(2):
                        moved[g][row:row + 8, 2 * at + h] = (
                            piece[h * 64:(h + 1) * 64].reshape(8, 8, 128).astype(jnp.bfloat16))
        for step in HALF_FAR_FIRST:
            other, device = half_partner(half, *step)
            if step == (0, 0, 0):
                @pl.when(low != half)
                def _():
                    send(moved[g].at[other], back[g].at[me], bwd_send.at[g, half], bwd_recv.at[g], device)

                @pl.when(low == half)
                def _():
                    pltpu.make_async_copy(moved[g].at[me], back[g].at[me], bwd_recv.at[g]).start()
            else:
                send(moved[g].at[other], back[g].at[me], bwd_send.at[g, half], bwd_recv.at[g], device)

    def finish(g):
        first, last = CHUNKS[g]
        landed(back[g], bwd_recv.at[g])
        matrix = turning_t[...]
        for at, s0 in enumerate(range(first, last, 2)):
            if s0 + 1 == last:
                block = back[g][:, 2 * at].reshape(256, 128)
                block = jnp.concatenate([block[:, :64], block[:, 64:]], axis=0)
                out_ref[s0] = nn(matrix, block).T.astype(jnp.bfloat16)
                continue
            block = jnp.concatenate([back[g][:, 2 * at + h].reshape(256, 128) for h in range(2)], axis=0)
            piece = nn(matrix, block).T.astype(jnp.bfloat16)
            for m in range(2):
                out_ref[s0 + m] = piece[m * 64:(m + 1) * 64]
        pltpu.make_async_copy(out_ref.at[first:last], out_hbm.at[first:last], out_sem.at[g]).start()

    loads[3].wait()
    for g in range(count):
        turn(g)
        if g == 0:
            @pl.when(jnp.logical_not(is_first))
            def _():
                pl.semaphore_wait(barrier, len(friends) - jnp.where(knows_first, 1, 0))
        spread(g)

    prepare_steps()
    prepare_return()
    greet_first()
    stages = {
        "b": rise, "a": sink, "y": lambda g: lay(got[g], 128, 4, g), "h": lambda g: translate(g, 1), "l": lambda g: translate(g, 0), "e": finish,
    }
    for token in ORDER:
        stages[token[0]](int(token[1:]))

    for g in range(count):
        landed(turned[g].at[pl.ds(0, 31)], fwd_send.at[g])
        landed(below[g], halo_send.at[g, 0])
        landed(above[g], halo_send.at[g, 1])
        for half in range(2):
            @pl.when(low == half)
            def _():
                landed(moved[g].at[pl.ds(0, 15)], bwd_send.at[g, half])

            @pl.when(low != half)
            def _():
                landed(moved[g].at[pl.ds(0, 16)], bwd_send.at[g, half])

    for g, (first, last) in enumerate(CHUNKS):
        landed(out_ref.at[first:last], out_sem.at[g])


def on_device(multipoles, rotation, coaxial, offsets, class_index):
    tables = jnp.asarray(block_tables(), jnp.bfloat16)
    rows = jnp.transpose(multipoles, (1, 0, 2))
    hbm = pl.BlockSpec(memory_space=pl.ANY)
    count = len(CHUNKS)
    bf16 = jnp.bfloat16
    scratch = []
    for outer in (32, 32, 16, 16, 32, 32):
        scratch += [pltpu.VMEM((outer, tiles(g), 8, 128), bf16) for g in range(count)]
    dma = pltpu.SemaphoreType.DMA
    scratch += [
        pltpu.SMEM((NCLASS * PER,), jnp.int32),
        pltpu.SMEM((NCLASS * PER,), jnp.int32),
        pltpu.VMEM((COMPONENTS, 64, 128), bf16),
        pltpu.VMEM((COMPONENTS, 64, 128), bf16),
        pltpu.VMEM((COMPONENTS, 512, 128), jnp.float32),
        pltpu.VMEM((4, 128, 128), bf16),
        pltpu.VMEM((NCLASS, 1, 128, 128), bf16),
        pltpu.VMEM((NCLASS * PER, 1, 128, 128), bf16),
        pltpu.VMEM((NCLASS * 128, 128), bf16),
        pltpu.VMEM((128, NCLASS * 128), bf16),
        pltpu.VMEM((PER, 128, 128), bf16),
        pltpu.SMEM((PER,), jnp.int32),
        dma((6,)), dma((count,)), pltpu.SemaphoreType.REGULAR,
        dma((count,)), dma((count, 2)),
        dma((count, 2)), dma((count, 2)),
        dma((count, 2)), dma((count,)),
    ]
    field = pl.pallas_call(
        kernel,
        out_shape=jax.ShapeDtypeStruct((COMPONENTS, 64, 128), bf16),
        in_specs=[hbm] * 6,
        out_specs=hbm,
        scratch_shapes=scratch,
        compiler_params=pltpu.CompilerParams(collective_id=0, has_side_effects=True),
        name="multipole_to_local",
    )(rows, tables, rotation, coaxial, offsets, class_index)
    return jnp.transpose(field, (1, 0, 2))


def solution(mesh):
    placed = (
        P("cell", None, "coef"),
        P(None, "coef", None, None),
        P(None, "coef", None, None),
        P(),
        P(),
    )
    return jax.shard_map(
        on_device, mesh=mesh, in_specs=placed, out_specs=P("cell", None, "coef"), check_vma=False
    )
```

```python
import jax
import jax.numpy as jnp
import numpy as np
from jax import lax
from jax.experimental import pallas as pl
from jax.experimental.pallas import tpu as pltpu
from jax.sharding import PartitionSpec as P

NCLASS = 4
PER = 10
COMPONENTS = 9
CHUNKS = ((0, 2), (2, 6), (6, 9))
ORDER = (
    "b0", "a0", "y0", "b1", "a1", "y1", "h0", "b2", "a2", "l0",
    "h1", "y2", "l1", "h2", "l2", "e0", "e1", "e2",
)
MESH = pl.DeviceIdType.MESH


def far_first():
    ways = {}
    for dx in range(4):
        for dy in range(4):
            for dc in range(2):
                if (dx, dy, dc) != (0, 0, 0):
                    ways.setdefault((dx, dy), []).append((dx, dy, dc))
    hops = lambda way: min(way[0], 4 - way[0]) + min(way[1], 4 - way[1])
    keys = sorted(ways, key=lambda way: -hops(way))
    return [ways[key][-1 - turn] for turn in range(2) for key in keys if turn < len(ways[key])]


FAR_FIRST = far_first()
HALF_FAR_FIRST = [
    (dx, dh, dc) for dc in (1, 0) for dx, dh in (
        (2, 1), (2, 0), (1, 1), (3, 1), (0, 1), (1, 0), (3, 0), (0, 0))]


def block_tables():
    degree_list = []
    for block_number in range(8):
        for level in (block_number, 15 - block_number, 16 + block_number, 31 - block_number):
            for order in range(-level, level + 1):
                degree_list.append((level, order))
    order_list = []
    for block_number in range(8):
        if block_number == 0:
            magnitudes = (0, 16, 8, 24)
        else:
            magnitudes = (block_number, 32 - block_number, 16 - block_number, 16 + block_number)
        for size_m in magnitudes:
            for order in [size_m] if size_m == 0 else [size_m, -size_m]:
                for level in range(size_m, 32):
                    order_list.append((level, order))
    where_degree = {pair: index for index, pair in enumerate(degree_list)}
    by_degree = np.zeros((8, 128, 128), np.float32)
    by_order = np.zeros((8, 128, 128), np.float32)
    filled = np.zeros((8, 8), np.int32)
    for order_at, pair in enumerate(order_list):
        degree_at = where_degree[pair]
        a, b = degree_at // 128, order_at // 128
        slot = filled[a, b]
        filled[a, b] += 1
        by_degree[a, b * 16 + slot, degree_at % 128] = 1.0
        by_order[b, (slot // 8) * 64 + a * 8 + slot % 8, order_at % 128] = 1.0
    assert (filled == 16).all()
    levels = np.array([pair[0] for pair in degree_list]).reshape(8, 128)
    orders = np.array([pair[1] for pair in order_list]).reshape(8, 128)
    same_level = (levels[:, :, None] == levels[:, None, :]).astype(np.float32)
    same_order = (orders[:, :, None] == orders[:, None, :]).astype(np.float32)
    return np.stack([by_degree, by_order, same_level, same_order], axis=1)


def tiles(g):
    return CHUNKS[g][1] - CHUNKS[g][0]


def nt(left, right):
    return lax.dot_general(left, right, (((1,), (1,)), ((), ())), preferred_element_type=jnp.float32)


def nn(left, right):
    return jnp.dot(left, right, preferred_element_type=jnp.float32)


def halves_first(rows):
    count, width = rows.shape[0] // 16, rows.shape[1]
    split = rows.reshape(count, 2, 8, width)
    return jnp.concatenate([split[:, h].reshape(count * 8, width) for h in range(2)], axis=0)


def kernel(x_hbm, tables_hbm, rot_hbm, coax_hbm, offs_hbm, cls_hbm, out_ref, *scratch):
    count = len(CHUNKS)
    names = ("turned", "got", "below", "above", "moved", "back")
    buffers = {name: scratch[i * count:(i + 1) * count] for i, name in enumerate(names)}
    turned, got, below, above, moved, back = (buffers[name] for name in names)
    (offs_ref, cls_ref, x_ref, cells, tables, rot, coax, turning, turning_t, steps, chosen, load_sem, late_sem,
     fwd_send, fwd_recv, halo_send, halo_recv, bwd_send, bwd_recv) = scratch[len(names) * count:]
    cell = lax.axis_index("cell")
    coef = lax.axis_index("coef")
    cell_total = lax.axis_size("cell")
    part = cell % 4
    plane = cell - part
    me = part * 8 + coef
    along, high, low, core = coef % 4, coef // 4, part // 2, part % 2
    up = (cell + 4) % cell_total
    down = (cell + cell_total - 4) % cell_total
    is_first = jnp.logical_and(cell == 0, coef == 0)
    beside_first = jnp.logical_and(coef == 0, jnp.logical_or(up == 0, down == 0))
    knows_first = jnp.logical_and(
        jnp.logical_not(is_first), jnp.logical_or(plane == 0, beside_first))

    xs = [(along + i) % 4 for i in range(4)]
    ys = [(high * 2 + low + i) % 4 for i in range(4)]
    cores = [core, 1 - core]

    def partner(dx, dy, dc):
        to_part = (ys[dy] % 2) * 2 + cores[dc]
        to_coef = (ys[dy] // 2) * 4 + xs[dx]
        return to_part * 8 + to_coef, (plane + to_part, to_coef)

    def half_partner(half, dx, dh, dc):
        to_part = half * 2 + cores[dc]
        to_coef = (high + dh) % 2 * 4 + xs[dx]
        return to_part * 8 + to_coef, (plane + to_part, to_coef)

    barrier = pltpu.get_barrier_semaphore()
    friends = [partner(*step)[1] for step in FAR_FIRST] + [(up, coef), (down, coef)]

    @pl.when(jnp.logical_not(is_first))
    def _():
        for device in friends:
            pl.semaphore_signal(barrier, inc=1, device_id=device, device_id_type=MESH)

    loads = [
        pltpu.make_async_copy(tables_hbm.at[coef], tables, load_sem.at[0]),
        pltpu.make_async_copy(rot_hbm, rot, load_sem.at[1]),
        pltpu.make_async_copy(coax_hbm, coax, load_sem.at[2]),
        pltpu.make_async_copy(x_hbm, x_ref, load_sem.at[3]),
        pltpu.make_async_copy(offs_hbm, offs_ref, load_sem.at[4]),
        pltpu.make_async_copy(cls_hbm, cls_ref, load_sem.at[5]),
    ]
    for load in (loads[0], loads[1], loads[3], loads[2], loads[4], loads[5]):
        load.start()

    @pl.when(is_first)
    def _():
        pl.semaphore_wait(barrier, len(friends))
        for device in friends:
            pl.semaphore_signal(late_sem, inc=1, device_id=device, device_id_type=MESH)

    loads[0].wait()
    loads[1].wait()
    for c in range(NCLASS):
        masked = rot[c, 0] * tables[2]
        turning[c * 128:(c + 1) * 128, :] = nn(tables[0], masked).astype(jnp.bfloat16)

    def send(source, target, send_sem, recv_sem, device):
        pltpu.make_async_remote_copy(
            source, target, send_sem, recv_sem, device_id=device, device_id_type=MESH).start()

    def landed(ref, sem):
        pltpu.make_async_copy(ref, ref, sem).wait()

    def turn(g):
        first, last = CHUNKS[g]
        for at, s0 in enumerate(range(first, last, 2)):
            members = range(s0, min(s0 + 2, last))
            rows = x_ref[s0:members[-1] + 1].reshape(len(members) * 64, 128)
            result = nt(turning[...], rows).reshape(32, 2, 8, len(members) * 64)
            if len(members) == 1:
                result = jnp.concatenate([result[:, 0], result[:, 1]], axis=2)
                turned[g][:, 2 * at] = result.astype(jnp.bfloat16)
            else:
                for h in range(2):
                    turned[g][:, 2 * at + h] = result[:, h].astype(jnp.bfloat16)

    def spread(g):
        for step in FAR_FIRST:
            other, device = partner(*step)

            @pl.when(jnp.logical_or(plane != 0, other != 0))
            def _():
                send(turned[g].at[other], got[g].at[me], fwd_send.at[g], fwd_recv.at[g, low], device)

        pltpu.make_async_copy(turned[g].at[me], got[g].at[me], fwd_recv.at[g, low]).start()

    def greet_first():
        @pl.when(knows_first)
        def _():
            pl.semaphore_wait(late_sem, 1)

        @pl.when(jnp.logical_and(knows_first, plane == 0))
        def _():
            for g in range(count):
                send(turned[g].at[0], got[g].at[me], fwd_send.at[g], fwd_recv.at[g, low], (0, 0))

    def pick(k, carry):
        seen, kept = carry[0], carry[1:]
        hit = cls_ref[k] == part
        kept = tuple(
            jnp.where(jnp.logical_and(hit, seen == p), k, old) for p, old in enumerate(kept))
        return (seen + jnp.where(hit, 1, 0),) + kept

    def prepare_steps():
        loads[4].wait()
        loads[5].wait()
        picked = lax.fori_loop(0, NCLASS * PER, pick, (jnp.int32(0),) * (PER + 1))[1:]
        for p in range(PER):
            chosen[p] = picked[p]
        loads[2].wait()

        def prepare(p, carry):
            masked = coax[chosen[p], 0] * tables[3]
            half = nn(tables[1], masked).astype(jnp.bfloat16)
            steps[p] = nt(half, tables[1]).astype(jnp.bfloat16)
            return carry

        lax.fori_loop(0, PER, prepare, 0)

    def prepare_return():
        rows = halves_first(turning[...].astype(jnp.float32))
        for c in range(NCLASS):
            turning_t[:, c * 128:(c + 1) * 128] = rows[c * 128:(c + 1) * 128].T.astype(jnp.bfloat16)

    def lay(buffer, row, groups, g):
        first, last = CHUNKS[g]
        for j in range(groups):
            for at, s0 in enumerate(range(first, last, 2)):
                if s0 + 1 == last:
                    block = buffer[j * 8:(j + 1) * 8, 2 * at].astype(jnp.float32).reshape(64, 128).T
                    cells[s0, row + j * 64:row + j * 64 + 64, :] = jnp.concatenate(
                        [block[:64], block[64:]], axis=1)
                    continue
                block = jnp.concatenate(
                    [buffer[j * 8:(j + 1) * 8, 2 * at + h].astype(jnp.float32).reshape(64, 128)
                     for h in range(2)], axis=0).T
                for m in range(2):
                    cells[s0 + m, row + j * 64:row + j * 64 + 64, :] = block[m * 64:(m + 1) * 64]

    def rise(g):
        upper = got[g].at[pl.ds(16, 16)]
        landed(upper, fwd_recv.at[g, 1])
        send(upper, below[g], halo_send.at[g, 0], halo_recv.at[g, 0], (up, coef))

    def sink(g):
        lower = got[g].at[pl.ds(0, 16)]
        landed(lower, fwd_recv.at[g, 0])
        send(lower, above[g], halo_send.at[g, 1], halo_recv.at[g, 1], (down, coef))

    def translate(g, half):
        first, last = CHUNKS[g]
        if half:
            landed(above[g], halo_recv.at[g, 1])
            lay(above[g], 384, 2, g)
        else:
            landed(below[g], halo_recv.at[g, 0])
            lay(below[g], 0, 2, g)
        matrices = jnp.concatenate([steps[p] for p in range(PER)], axis=1)
        starts = [128 + half * 128 + offs_ref[chosen[p]] for p in range(PER)]
        for at, s0 in enumerate(range(first, last, 2)):
            members = range(s0, min(s0 + 2, last))
            width = 64 * len(members)
            pieces = []
            for p in range(PER):
                pieces.append(jnp.concatenate(
                    [cells[s, pl.ds(starts[p] + i * 64, 64), :] for i in range(2) for s in members],
                    axis=0).astype(jnp.bfloat16))
            result = nt(matrices, jnp.concatenate(pieces, axis=1))
            for i in range(2):
                row = (half * 2 + i) * 8
                piece = result[:, i * width:(i + 1) * width]
                if len(members) == 1:
                    piece = jnp.concatenate([piece[:64], piece[64:]], axis=1)
                    moved[g][row:row + 8, 2 * at] = piece.reshape(8, 8, 128).astype(jnp.bfloat16)
                else:
                    for h in range(2):
                        moved[g][row:row + 8, 2 * at + h] = (
                            piece[h * 64:(h + 1) * 64].reshape(8, 8, 128).astype(jnp.bfloat16))
        for step in HALF_FAR_FIRST:
            other, device = half_partner(half, *step)
            if step == (0, 0, 0):
                @pl.when(low != half)
                def _():
                    send(moved[g].at[other], back[g].at[me], bwd_send.at[g, half], bwd_recv.at[g], device)

                @pl.when(low == half)
                def _():
                    pltpu.make_async_copy(moved[g].at[me], back[g].at[me], bwd_recv.at[g]).start()
            else:
                send(moved[g].at[other], back[g].at[me], bwd_send.at[g, half], bwd_recv.at[g], device)

    def finish(g):
        first, last = CHUNKS[g]
        landed(back[g], bwd_recv.at[g])
        matrix = turning_t[...]
        for at, s0 in enumerate(range(first, last, 2)):
            if s0 + 1 == last:
                block = back[g][:, 2 * at].reshape(256, 128)
                block = jnp.concatenate([block[:, :64], block[:, 64:]], axis=0)
                out_ref[s0] = nn(matrix, block).T.astype(jnp.bfloat16)
                continue
            block = jnp.concatenate([back[g][:, 2 * at + h].reshape(256, 128) for h in range(2)], axis=0)
            piece = nn(matrix, block).T.astype(jnp.bfloat16)
            for m in range(2):
                out_ref[s0 + m] = piece[m * 64:(m + 1) * 64]

    loads[3].wait()
    for g in range(count):
        turn(g)
        if g == 0:
            @pl.when(jnp.logical_not(is_first))
            def _():
                pl.semaphore_wait(barrier, len(friends) - jnp.where(knows_first, 1, 0))
        spread(g)

    prepare_steps()
    prepare_return()
    greet_first()
    stages = {
        "b": rise, "a": sink, "y": lambda g: lay(got[g], 128, 4, g), "h": lambda g: translate(g, 1), "l": lambda g: translate(g, 0), "e": finish,
    }
    for token in ORDER:
        stages[token[0]](int(token[1:]))

    for g in range(count):
        landed(turned[g].at[pl.ds(0, 31)], fwd_send.at[g])
        landed(below[g], halo_send.at[g, 0])
        landed(above[g], halo_send.at[g, 1])
        for half in range(2):
            @pl.when(low == half)
            def _():
                landed(moved[g].at[pl.ds(0, 15)], bwd_send.at[g, half])

            @pl.when(low != half)
            def _():
                landed(moved[g].at[pl.ds(0, 16)], bwd_send.at[g, half])

def on_device(multipoles, rotation, coaxial, offsets, class_index):
    tables = jnp.asarray(block_tables(), jnp.bfloat16)
    rows = jnp.transpose(multipoles, (1, 0, 2))
    hbm = pl.BlockSpec(memory_space=pl.ANY)
    count = len(CHUNKS)
    bf16 = jnp.bfloat16
    scratch = []
    for outer in (32, 32, 16, 16, 32, 32):
        scratch += [pltpu.VMEM((outer, tiles(g), 8, 128), bf16) for g in range(count)]
    dma = pltpu.SemaphoreType.DMA
    scratch += [
        pltpu.SMEM((NCLASS * PER,), jnp.int32),
        pltpu.SMEM((NCLASS * PER,), jnp.int32),
        pltpu.VMEM((COMPONENTS, 64, 128), bf16),
        pltpu.VMEM((COMPONENTS, 512, 128), jnp.float32),
        pltpu.VMEM((4, 128, 128), bf16),
        pltpu.VMEM((NCLASS, 1, 128, 128), bf16),
        pltpu.VMEM((NCLASS * PER, 1, 128, 128), bf16),
        pltpu.VMEM((NCLASS * 128, 128), bf16),
        pltpu.VMEM((128, NCLASS * 128), bf16),
        pltpu.VMEM((PER, 128, 128), bf16),
        pltpu.SMEM((PER,), jnp.int32),
        dma((6,)), pltpu.SemaphoreType.REGULAR,
        dma((count,)), dma((count, 2)),
        dma((count, 2)), dma((count, 2)),
        dma((count, 2)), dma((count,)),
    ]
    field = pl.pallas_call(
        kernel,
        out_shape=pltpu.VMEM((COMPONENTS, 64, 128), bf16),
        in_specs=[hbm] * 6,
        out_specs=pl.BlockSpec(memory_space=pltpu.VMEM),
        scratch_shapes=scratch,
        compiler_params=pltpu.CompilerParams(collective_id=0, has_side_effects=True),
        name="multipole_to_local",
    )(rows, tables, rotation, coaxial, offsets, class_index)
    return jnp.transpose(field, (1, 0, 2))


def solution(mesh):
    placed = (
        P("cell", None, "coef"),
        P(None, "coef", None, None),
        P(None, "coef", None, None),
        P(),
        P(),
    )
    return jax.shard_map(
        on_device, mesh=mesh, in_specs=placed, out_specs=P("cell", None, "coef"), check_vma=False
    )
```

```python
import jax
import jax.numpy as jnp
import numpy as np
from jax import lax
from jax.experimental import pallas as pl
from jax.experimental.pallas import tpu as pltpu
from jax.sharding import PartitionSpec as P

NCLASS = 4
PER = 10
COMPONENTS = 9
CHUNKS = ((0, 2), (2, 6), (6, 9))
ORDER = (
    "b0", "a0", "y0", "b1", "a1", "b2", "a2", "y1", "h0", "h1", "l0", "y2", "h2", "l1", "l2", "e0", "e1", "e2",
)
MESH = pl.DeviceIdType.MESH


def far_first():
    ways = {}
    for dx in range(4):
        for dy in range(4):
            for dc in range(2):
                if (dx, dy, dc) != (0, 0, 0):
                    ways.setdefault((dx, dy), []).append((dx, dy, dc))
    hops = lambda way: min(way[0], 4 - way[0]) + min(way[1], 4 - way[1])
    keys = sorted(ways, key=lambda way: -hops(way))
    return [ways[key][-1 - turn] for turn in range(2) for key in keys if turn < len(ways[key])]


FAR_FIRST = far_first()
HALF_FAR_FIRST = [
    (dx, dh, dc) for dc in (1, 0) for dx, dh in (
        (2, 1), (2, 0), (1, 1), (3, 1), (0, 1), (1, 0), (3, 0), (0, 0))]


def block_tables():
    degree_list = []
    for block_number in range(8):
        for level in (block_number, 15 - block_number, 16 + block_number, 31 - block_number):
            for order in range(-level, level + 1):
                degree_list.append((level, order))
    order_list = []
    for block_number in range(8):
        if block_number == 0:
            magnitudes = (0, 16, 8, 24)
        else:
            magnitudes = (block_number, 32 - block_number, 16 - block_number, 16 + block_number)
        for size_m in magnitudes:
            for order in [size_m] if size_m == 0 else [size_m, -size_m]:
                for level in range(size_m, 32):
                    order_list.append((level, order))
    where_degree = {pair: index for index, pair in enumerate(degree_list)}
    by_degree = np.zeros((8, 128, 128), np.float32)
    by_order = np.zeros((8, 128, 128), np.float32)
    filled = np.zeros((8, 8), np.int32)
    for order_at, pair in enumerate(order_list):
        degree_at = where_degree[pair]
        a, b = degree_at // 128, order_at // 128
        slot = filled[a, b]
        filled[a, b] += 1
        by_degree[a, b * 16 + slot, degree_at % 128] = 1.0
        by_order[b, (slot // 8) * 64 + a * 8 + slot % 8, order_at % 128] = 1.0
    assert (filled == 16).all()
    levels = np.array([pair[0] for pair in degree_list]).reshape(8, 128)
    orders = np.array([pair[1] for pair in order_list]).reshape(8, 128)
    same_level = (levels[:, :, None] == levels[:, None, :]).astype(np.float32)
    same_order = (orders[:, :, None] == orders[:, None, :]).astype(np.float32)
    return np.stack([by_degree, by_order, same_level, same_order], axis=1)


def tiles(g):
    return CHUNKS[g][1] - CHUNKS[g][0]


def nt(left, right):
    return lax.dot_general(left, right, (((1,), (1,)), ((), ())), preferred_element_type=jnp.float32)


def nn(left, right):
    return jnp.dot(left, right, preferred_element_type=jnp.float32)


def halves_first(rows):
    count, width = rows.shape[0] // 16, rows.shape[1]
    split = rows.reshape(count, 2, 8, width)
    return jnp.concatenate([split[:, h].reshape(count * 8, width) for h in range(2)], axis=0)


def kernel(x_hbm, tables_hbm, rot_hbm, coax_hbm, offs_hbm, cls_hbm, out_ref, *scratch):
    count = len(CHUNKS)
    names = ("turned", "got", "below", "above", "moved", "back")
    buffers = {name: scratch[i * count:(i + 1) * count] for i, name in enumerate(names)}
    turned, got, below, above, moved, back = (buffers[name] for name in names)
    (offs_ref, cls_ref, x_ref, cells, tables, rot, coax, turning, turning_t, steps, chosen, load_sem, late_sem,
     fwd_send, fwd_recv, halo_send, halo_recv, bwd_send, bwd_recv) = scratch[len(names) * count:]
    cell = lax.axis_index("cell")
    coef = lax.axis_index("coef")
    cell_total = lax.axis_size("cell")
    part = cell % 4
    plane = cell - part
    me = part * 8 + coef
    along, high, low, core = coef % 4, coef // 4, part // 2, part % 2
    up = (cell + 4) % cell_total
    down = (cell + cell_total - 4) % cell_total
    is_first = jnp.logical_and(cell == 0, coef == 0)
    beside_first = jnp.logical_and(coef == 0, jnp.logical_or(up == 0, down == 0))
    knows_first = jnp.logical_and(
        jnp.logical_not(is_first), jnp.logical_or(plane == 0, beside_first))

    xs = [(along + i) % 4 for i in range(4)]
    ys = [(high * 2 + low + i) % 4 for i in range(4)]
    cores = [core, 1 - core]

    def partner(dx, dy, dc):
        to_part = (ys[dy] % 2) * 2 + cores[dc]
        to_coef = (ys[dy] // 2) * 4 + xs[dx]
        return to_part * 8 + to_coef, (plane + to_part, to_coef)

    def half_partner(half, dx, dh, dc):
        to_part = half * 2 + cores[dc]
        to_coef = (high + dh) % 2 * 4 + xs[dx]
        return to_part * 8 + to_coef, (plane + to_part, to_coef)

    barrier = pltpu.get_barrier_semaphore()
    friends = [partner(*step)[1] for step in FAR_FIRST] + [(up, coef), (down, coef)]

    @pl.when(jnp.logical_not(is_first))
    def _():
        for device in friends:
            pl.semaphore_signal(barrier, inc=1, device_id=device, device_id_type=MESH)

    loads = [
        pltpu.make_async_copy(tables_hbm.at[coef], tables, load_sem.at[0]),
        pltpu.make_async_copy(rot_hbm, rot, load_sem.at[1]),
        pltpu.make_async_copy(coax_hbm, coax, load_sem.at[2]),
        pltpu.make_async_copy(x_hbm, x_ref, load_sem.at[3]),
        pltpu.make_async_copy(offs_hbm, offs_ref, load_sem.at[4]),
        pltpu.make_async_copy(cls_hbm, cls_ref, load_sem.at[5]),
    ]
    for load in (loads[0], loads[1], loads[3], loads[2], loads[4], loads[5]):
        load.start()

    @pl.when(is_first)
    def _():
        pl.semaphore_wait(barrier, len(friends))
        for device in friends:
            pl.semaphore_signal(late_sem, inc=1, device_id=device, device_id_type=MESH)

    loads[0].wait()
    loads[1].wait()
    for c in range(NCLASS):
        masked = rot[c, 0] * tables[2]
        turning[c * 128:(c + 1) * 128, :] = nn(tables[0], masked).astype(jnp.bfloat16)

    def send(source, target, send_sem, recv_sem, device):
        pltpu.make_async_remote_copy(
            source, target, send_sem, recv_sem, device_id=device, device_id_type=MESH).start()

    def landed(ref, sem):
        pltpu.make_async_copy(ref, ref, sem).wait()

    def turn(g):
        first, last = CHUNKS[g]
        for at, s0 in enumerate(range(first, last, 2)):
            members = range(s0, min(s0 + 2, last))
            rows = x_ref[s0:members[-1] + 1].reshape(len(members) * 64, 128)
            result = nt(turning[...], rows).reshape(32, 2, 8, len(members) * 64)
            if len(members) == 1:
                result = jnp.concatenate([result[:, 0], result[:, 1]], axis=2)
                turned[g][:, 2 * at] = result.astype(jnp.bfloat16)
            else:
                for h in range(2):
                    turned[g][:, 2 * at + h] = result[:, h].astype(jnp.bfloat16)

    def spread(g):
        for step in FAR_FIRST:
            other, device = partner(*step)

            @pl.when(jnp.logical_or(plane != 0, other != 0))
            def _():
                send(turned[g].at[other], got[g].at[me], fwd_send.at[g], fwd_recv.at[g, low], device)

        pltpu.make_async_copy(turned[g].at[me], got[g].at[me], fwd_recv.at[g, low]).start()

    def greet_first():
        @pl.when(knows_first)
        def _():
            pl.semaphore_wait(late_sem, 1)

        @pl.when(jnp.logical_and(knows_first, plane == 0))
        def _():
            for g in range(count):
                send(turned[g].at[0], got[g].at[me], fwd_send.at[g], fwd_recv.at[g, low], (0, 0))

    def pick(k, carry):
        seen, kept = carry[0], carry[1:]
        hit = cls_ref[k] == part
        kept = tuple(
            jnp.where(jnp.logical_and(hit, seen == p), k, old) for p, old in enumerate(kept))
        return (seen + jnp.where(hit, 1, 0),) + kept

    def prepare_steps():
        loads[4].wait()
        loads[5].wait()
        picked = lax.fori_loop(0, NCLASS * PER, pick, (jnp.int32(0),) * (PER + 1))[1:]
        for p in range(PER):
            chosen[p] = picked[p]
        loads[2].wait()

        def prepare(p, carry):
            masked = coax[chosen[p], 0] * tables[3]
            half = nn(tables[1], masked).astype(jnp.bfloat16)
            steps[p] = nt(half, tables[1]).astype(jnp.bfloat16)
            return carry

        lax.fori_loop(0, PER, prepare, 0)

    def prepare_return():
        rows = halves_first(turning[...].astype(jnp.float32))
        for c in range(NCLASS):
            turning_t[:, c * 128:(c + 1) * 128] = rows[c * 128:(c + 1) * 128].T.astype(jnp.bfloat16)

    def lay(buffer, row, groups, g):
        first, last = CHUNKS[g]
        for j in range(groups):
            for at, s0 in enumerate(range(first, last, 2)):
                if s0 + 1 == last:
                    block = buffer[j * 8:(j + 1) * 8, 2 * at].astype(jnp.float32).reshape(64, 128).T
                    cells[s0, row + j * 64:row + j * 64 + 64, :] = jnp.concatenate(
                        [block[:64], block[64:]], axis=1)
                    continue
                block = jnp.concatenate(
                    [buffer[j * 8:(j + 1) * 8, 2 * at + h].astype(jnp.float32).reshape(64, 128)
                     for h in range(2)], axis=0).T
                for m in range(2):
                    cells[s0 + m, row + j * 64:row + j * 64 + 64, :] = block[m * 64:(m + 1) * 64]

    def rise(g):
        upper = got[g].at[pl.ds(16, 16)]
        landed(upper, fwd_recv.at[g, 1])
        send(upper, below[g], halo_send.at[g, 0], halo_recv.at[g, 0], (up, coef))

    def sink(g):
        lower = got[g].at[pl.ds(0, 16)]
        landed(lower, fwd_recv.at[g, 0])
        send(lower, above[g], halo_send.at[g, 1], halo_recv.at[g, 1], (down, coef))

    def translate(g, half):
        first, last = CHUNKS[g]
        if half:
            landed(above[g], halo_recv.at[g, 1])
            lay(above[g], 384, 2, g)
        else:
            landed(below[g], halo_recv.at[g, 0])
            lay(below[g], 0, 2, g)
        matrices = jnp.concatenate([steps[p] for p in range(PER)], axis=1)
        starts = [128 + half * 128 + offs_ref[chosen[p]] for p in range(PER)]
        for at, s0 in enumerate(range(first, last, 2)):
            members = range(s0, min(s0 + 2, last))
            width = 64 * len(members)
            pieces = []
            for p in range(PER):
                pieces.append(jnp.concatenate(
                    [cells[s, pl.ds(starts[p] + i * 64, 64), :] for i in range(2) for s in members],
                    axis=0).astype(jnp.bfloat16))
            result = nt(matrices, jnp.concatenate(pieces, axis=1))
            for i in range(2):
                row = (half * 2 + i) * 8
                piece = result[:, i * width:(i + 1) * width]
                if len(members) == 1:
                    piece = jnp.concatenate([piece[:64], piece[64:]], axis=1)
                    moved[g][row:row + 8, 2 * at] = piece.reshape(8, 8, 128).astype(jnp.bfloat16)
                else:
                    for h in range(2):
                        moved[g][row:row + 8, 2 * at + h] = (
                            piece[h * 64:(h + 1) * 64].reshape(8, 8, 128).astype(jnp.bfloat16))
        for step in HALF_FAR_FIRST:
            other, device = half_partner(half, *step)
            if step == (0, 0, 0):
                @pl.when(low != half)
                def _():
                    send(moved[g].at[other], back[g].at[me], bwd_send.at[g, half], bwd_recv.at[g], device)

                @pl.when(low == half)
                def _():
                    pltpu.make_async_copy(moved[g].at[me], back[g].at[me], bwd_recv.at[g]).start()
            else:
                send(moved[g].at[other], back[g].at[me], bwd_send.at[g, half], bwd_recv.at[g], device)

    def finish(g):
        first, last = CHUNKS[g]
        landed(back[g], bwd_recv.at[g])
        matrix = turning_t[...]
        for at, s0 in enumerate(range(first, last, 2)):
            if s0 + 1 == last:
                block = back[g][:, 2 * at].reshape(256, 128)
                block = jnp.concatenate([block[:, :64], block[:, 64:]], axis=0)
                out_ref[s0] = nn(matrix, block).T.astype(jnp.bfloat16)
                continue
            block = jnp.concatenate([back[g][:, 2 * at + h].reshape(256, 128) for h in range(2)], axis=0)
            piece = nn(matrix, block).T.astype(jnp.bfloat16)
            for m in range(2):
                out_ref[s0 + m] = piece[m * 64:(m + 1) * 64]

    loads[3].wait()
    for g in range(count):
        turn(g)
        if g == 0:
            @pl.when(jnp.logical_not(is_first))
            def _():
                pl.semaphore_wait(barrier, len(friends) - jnp.where(knows_first, 1, 0))
        spread(g)

    prepare_steps()
    prepare_return()
    greet_first()
    stages = {
        "b": rise, "a": sink, "y": lambda g: lay(got[g], 128, 4, g), "h": lambda g: translate(g, 1), "l": lambda g: translate(g, 0), "e": finish,
    }
    for token in ORDER:
        stages[token[0]](int(token[1:]))

    for g in range(count):
        landed(turned[g].at[pl.ds(0, 31)], fwd_send.at[g])
        landed(below[g], halo_send.at[g, 0])
        landed(above[g], halo_send.at[g, 1])
        for half in range(2):
            @pl.when(low == half)
            def _():
                landed(moved[g].at[pl.ds(0, 15)], bwd_send.at[g, half])

            @pl.when(low != half)
            def _():
                landed(moved[g].at[pl.ds(0, 16)], bwd_send.at[g, half])

def on_device(multipoles, rotation, coaxial, offsets, class_index):
    tables = jnp.asarray(block_tables(), jnp.bfloat16)
    rows = jnp.transpose(multipoles, (1, 0, 2))
    hbm = pl.BlockSpec(memory_space=pl.ANY)
    count = len(CHUNKS)
    bf16 = jnp.bfloat16
    scratch = []
    for outer in (32, 32, 16, 16, 32, 32):
        scratch += [pltpu.VMEM((outer, tiles(g), 8, 128), bf16) for g in range(count)]
    dma = pltpu.SemaphoreType.DMA
    scratch += [
        pltpu.SMEM((NCLASS * PER,), jnp.int32),
        pltpu.SMEM((NCLASS * PER,), jnp.int32),
        pltpu.VMEM((COMPONENTS, 64, 128), bf16),
        pltpu.VMEM((COMPONENTS, 512, 128), jnp.float32),
        pltpu.VMEM((4, 128, 128), bf16),
        pltpu.VMEM((NCLASS, 1, 128, 128), bf16),
        pltpu.VMEM((NCLASS * PER, 1, 128, 128), bf16),
        pltpu.VMEM((NCLASS * 128, 128), bf16),
        pltpu.VMEM((128, NCLASS * 128), bf16),
        pltpu.VMEM((PER, 128, 128), bf16),
        pltpu.SMEM((PER,), jnp.int32),
        dma((6,)), pltpu.SemaphoreType.REGULAR,
        dma((count,)), dma((count, 2)),
        dma((count, 2)), dma((count, 2)),
        dma((count, 2)), dma((count,)),
    ]
    field = pl.pallas_call(
        kernel,
        out_shape=pltpu.VMEM((COMPONENTS, 64, 128), bf16),
        in_specs=[hbm] * 6,
        out_specs=pl.BlockSpec(memory_space=pltpu.VMEM),
        scratch_shapes=scratch,
        compiler_params=pltpu.CompilerParams(collective_id=0, has_side_effects=True),
        name="multipole_to_local",
    )(rows, tables, rotation, coaxial, offsets, class_index)
    return jnp.transpose(field, (1, 0, 2))


def solution(mesh):
    placed = (
        P("cell", None, "coef"),
        P(None, "coef", None, None),
        P(None, "coef", None, None),
        P(),
        P(),
    )
    return jax.shard_map(
        on_device, mesh=mesh, in_specs=placed, out_specs=P("cell", None, "coef"), check_vma=False
    )
```

```python
import jax
import jax.numpy as jnp
import numpy as np
from jax import lax
from jax.experimental import pallas as pl
from jax.experimental.pallas import tpu as pltpu
from jax.sharding import PartitionSpec as P

NCLASS = 4
PER = 10
COMPONENTS = 9
CHUNKS = ((0, 3), (3, 7), (7, 9))
ORDER = (
    "b0", "a0", "y0", "b1", "a1", "b2", "a2", "y1", "h0", "h1", "l0", "y2", "h2", "l1", "l2", "e0", "e1", "e2",
)
MESH = pl.DeviceIdType.MESH


def far_first():
    ways = {}
    for dx in range(4):
        for dy in range(4):
            for dc in range(2):
                if (dx, dy, dc) != (0, 0, 0):
                    ways.setdefault((dx, dy), []).append((dx, dy, dc))
    hops = lambda way: min(way[0], 4 - way[0]) + min(way[1], 4 - way[1])
    keys = sorted(ways, key=lambda way: -hops(way))
    return [ways[key][-1 - turn] for turn in range(2) for key in keys if turn < len(ways[key])]


FAR_FIRST = far_first()
HALF_FAR_FIRST = [
    (dx, dh, dc) for dc in (1, 0) for dx, dh in (
        (2, 1), (2, 0), (1, 1), (3, 1), (0, 1), (1, 0), (3, 0), (0, 0))]


def block_tables():
    degree_list = []
    for block_number in range(8):
        for level in (block_number, 15 - block_number, 16 + block_number, 31 - block_number):
            for order in range(-level, level + 1):
                degree_list.append((level, order))
    order_list = []
    for block_number in range(8):
        if block_number == 0:
            magnitudes = (0, 16, 8, 24)
        else:
            magnitudes = (block_number, 32 - block_number, 16 - block_number, 16 + block_number)
        for size_m in magnitudes:
            for order in [size_m] if size_m == 0 else [size_m, -size_m]:
                for level in range(size_m, 32):
                    order_list.append((level, order))
    where_degree = {pair: index for index, pair in enumerate(degree_list)}
    by_degree = np.zeros((8, 128, 128), np.float32)
    by_order = np.zeros((8, 128, 128), np.float32)
    filled = np.zeros((8, 8), np.int32)
    for order_at, pair in enumerate(order_list):
        degree_at = where_degree[pair]
        a, b = degree_at // 128, order_at // 128
        slot = filled[a, b]
        filled[a, b] += 1
        by_degree[a, b * 16 + slot, degree_at % 128] = 1.0
        by_order[b, (slot // 8) * 64 + a * 8 + slot % 8, order_at % 128] = 1.0
    assert (filled == 16).all()
    levels = np.array([pair[0] for pair in degree_list]).reshape(8, 128)
    orders = np.array([pair[1] for pair in order_list]).reshape(8, 128)
    same_level = (levels[:, :, None] == levels[:, None, :]).astype(np.float32)
    same_order = (orders[:, :, None] == orders[:, None, :]).astype(np.float32)
    return np.stack([by_degree, by_order, same_level, same_order], axis=1)


def tiles(g):
    return CHUNKS[g][1] - CHUNKS[g][0]


def nt(left, right):
    return lax.dot_general(left, right, (((1,), (1,)), ((), ())), preferred_element_type=jnp.float32)


def nn(left, right):
    return jnp.dot(left, right, preferred_element_type=jnp.float32)


def halves_first(rows):
    count, width = rows.shape[0] // 16, rows.shape[1]
    split = rows.reshape(count, 2, 8, width)
    return jnp.concatenate([split[:, h].reshape(count * 8, width) for h in range(2)], axis=0)


def kernel(x_hbm, tables_hbm, rot_hbm, coax_hbm, offs_hbm, cls_hbm, out_ref, *scratch):
    count = len(CHUNKS)
    names = ("turned", "got", "below", "above", "moved", "back")
    buffers = {name: scratch[i * count:(i + 1) * count] for i, name in enumerate(names)}
    turned, got, below, above, moved, back = (buffers[name] for name in names)
    (offs_ref, cls_ref, x_ref, cells, tables, rot, coax, turning, turning_t, steps, chosen, load_sem, late_sem,
     fwd_send, fwd_recv, halo_send, halo_recv, bwd_send, bwd_recv) = scratch[len(names) * count:]
    cell = lax.axis_index("cell")
    coef = lax.axis_index("coef")
    cell_total = lax.axis_size("cell")
    part = cell % 4
    plane = cell - part
    me = part * 8 + coef
    along, high, low, core = coef % 4, coef // 4, part // 2, part % 2
    up = (cell + 4) % cell_total
    down = (cell + cell_total - 4) % cell_total
    is_first = jnp.logical_and(cell == 0, coef == 0)
    beside_first = jnp.logical_and(coef == 0, jnp.logical_or(up == 0, down == 0))
    knows_first = jnp.logical_and(
        jnp.logical_not(is_first), jnp.logical_or(plane == 0, beside_first))

    xs = [(along + i) % 4 for i in range(4)]
    ys = [(high * 2 + low + i) % 4 for i in range(4)]
    cores = [core, 1 - core]

    def partner(dx, dy, dc):
        to_part = (ys[dy] % 2) * 2 + cores[dc]
        to_coef = (ys[dy] // 2) * 4 + xs[dx]
        return to_part * 8 + to_coef, (plane + to_part, to_coef)

    def half_partner(half, dx, dh, dc):
        to_part = half * 2 + cores[dc]
        to_coef = (high + dh) % 2 * 4 + xs[dx]
        return to_part * 8 + to_coef, (plane + to_part, to_coef)

    barrier = pltpu.get_barrier_semaphore()
    friends = [partner(*step)[1] for step in FAR_FIRST] + [(up, coef), (down, coef)]

    @pl.when(jnp.logical_not(is_first))
    def _():
        for device in friends:
            pl.semaphore_signal(barrier, inc=1, device_id=device, device_id_type=MESH)

    loads = [
        pltpu.make_async_copy(tables_hbm.at[coef], tables, load_sem.at[0]),
        pltpu.make_async_copy(rot_hbm, rot, load_sem.at[1]),
        pltpu.make_async_copy(coax_hbm, coax, load_sem.at[2]),
        pltpu.make_async_copy(x_hbm, x_ref, load_sem.at[3]),
        pltpu.make_async_copy(offs_hbm, offs_ref, load_sem.at[4]),
        pltpu.make_async_copy(cls_hbm, cls_ref, load_sem.at[5]),
    ]
    for load in (loads[0], loads[1], loads[3], loads[2], loads[4], loads[5]):
        load.start()

    @pl.when(is_first)
    def _():
        pl.semaphore_wait(barrier, len(friends))
        for device in friends:
            pl.semaphore_signal(late_sem, inc=1, device_id=device, device_id_type=MESH)

    loads[0].wait()
    loads[1].wait()
    for c in range(NCLASS):
        masked = rot[c, 0] * tables[2]
        turning[c * 128:(c + 1) * 128, :] = nn(tables[0], masked).astype(jnp.bfloat16)

    def send(source, target, send_sem, recv_sem, device):
        pltpu.make_async_remote_copy(
            source, target, send_sem, recv_sem, device_id=device, device_id_type=MESH).start()

    def landed(ref, sem):
        pltpu.make_async_copy(ref, ref, sem).wait()

    def turn(g):
        first, last = CHUNKS[g]
        for at, s0 in enumerate(range(first, last, 2)):
            members = range(s0, min(s0 + 2, last))
            rows = x_ref[s0:members[-1] + 1].reshape(len(members) * 64, 128)
            result = nt(turning[...], rows).reshape(32, 2, 8, len(members) * 64)
            if len(members) == 1:
                result = jnp.concatenate([result[:, 0], result[:, 1]], axis=2)
                turned[g][:, 2 * at] = result.astype(jnp.bfloat16)
            else:
                for h in range(2):
                    turned[g][:, 2 * at + h] = result[:, h].astype(jnp.bfloat16)

    def spread(g):
        for step in FAR_FIRST:
            other, device = partner(*step)

            @pl.when(jnp.logical_or(plane != 0, other != 0))
            def _():
                send(turned[g].at[other], got[g].at[me], fwd_send.at[g], fwd_recv.at[g, low], device)

        pltpu.make_async_copy(turned[g].at[me], got[g].at[me], fwd_recv.at[g, low]).start()

    def greet_first():
        @pl.when(knows_first)
        def _():
            pl.semaphore_wait(late_sem, 1)

        @pl.when(jnp.logical_and(knows_first, plane == 0))
        def _():
            for g in range(count):
                send(turned[g].at[0], got[g].at[me], fwd_send.at[g], fwd_recv.at[g, low], (0, 0))

    def pick(k, carry):
        seen, kept = carry[0], carry[1:]
        hit = cls_ref[k] == part
        kept = tuple(
            jnp.where(jnp.logical_and(hit, seen == p), k, old) for p, old in enumerate(kept))
        return (seen + jnp.where(hit, 1, 0),) + kept

    def prepare_steps():
        loads[4].wait()
        loads[5].wait()
        picked = lax.fori_loop(0, NCLASS * PER, pick, (jnp.int32(0),) * (PER + 1))[1:]
        for p in range(PER):
            chosen[p] = picked[p]
        loads[2].wait()

        def prepare(p, carry):
            masked = coax[chosen[p], 0] * tables[3]
            half = nn(tables[1], masked).astype(jnp.bfloat16)
            steps[p] = nt(half, tables[1]).astype(jnp.bfloat16)
            return carry

        lax.fori_loop(0, PER, prepare, 0)

    def prepare_return():
        rows = halves_first(turning[...].astype(jnp.float32))
        for c in range(NCLASS):
            turning_t[:, c * 128:(c + 1) * 128] = rows[c * 128:(c + 1) * 128].T.astype(jnp.bfloat16)

    def lay(buffer, row, groups, g):
        first, last = CHUNKS[g]
        for j in range(groups):
            for at, s0 in enumerate(range(first, last, 2)):
                if s0 + 1 == last:
                    block = buffer[j * 8:(j + 1) * 8, 2 * at].astype(jnp.float32).reshape(64, 128).T
                    cells[s0, row + j * 64:row + j * 64 + 64, :] = jnp.concatenate(
                        [block[:64], block[64:]], axis=1)
                    continue
                block = jnp.concatenate(
                    [buffer[j * 8:(j + 1) * 8, 2 * at + h].astype(jnp.float32).reshape(64, 128)
                     for h in range(2)], axis=0).T
                for m in range(2):
                    cells[s0 + m, row + j * 64:row + j * 64 + 64, :] = block[m * 64:(m + 1) * 64]

    def rise(g):
        upper = got[g].at[pl.ds(16, 16)]
        landed(upper, fwd_recv.at[g, 1])
        send(upper, below[g], halo_send.at[g, 0], halo_recv.at[g, 0], (up, coef))

    def sink(g):
        lower = got[g].at[pl.ds(0, 16)]
        landed(lower, fwd_recv.at[g, 0])
        send(lower, above[g], halo_send.at[g, 1], halo_recv.at[g, 1], (down, coef))

    def translate(g, half):
        first, last = CHUNKS[g]
        if half:
            landed(above[g], halo_recv.at[g, 1])
            lay(above[g], 384, 2, g)
        else:
            landed(below[g], halo_recv.at[g, 0])
            lay(below[g], 0, 2, g)
        matrices = jnp.concatenate([steps[p] for p in range(PER)], axis=1)
        starts = [128 + half * 128 + offs_ref[chosen[p]] for p in range(PER)]
        for at, s0 in enumerate(range(first, last, 2)):
            members = range(s0, min(s0 + 2, last))
            width = 64 * len(members)
            pieces = []
            for p in range(PER):
                pieces.append(jnp.concatenate(
                    [cells[s, pl.ds(starts[p] + i * 64, 64), :] for i in range(2) for s in members],
                    axis=0).astype(jnp.bfloat16))
            result = nt(matrices, jnp.concatenate(pieces, axis=1))
            for i in range(2):
                row = (half * 2 + i) * 8
                piece = result[:, i * width:(i + 1) * width]
                if len(members) == 1:
                    piece = jnp.concatenate([piece[:64], piece[64:]], axis=1)
                    moved[g][row:row + 8, 2 * at] = piece.reshape(8, 8, 128).astype(jnp.bfloat16)
                else:
                    for h in range(2):
                        moved[g][row:row + 8, 2 * at + h] = (
                            piece[h * 64:(h + 1) * 64].reshape(8, 8, 128).astype(jnp.bfloat16))
        for step in HALF_FAR_FIRST:
            other, device = half_partner(half, *step)
            if step == (0, 0, 0):
                @pl.when(low != half)
                def _():
                    send(moved[g].at[other], back[g].at[me], bwd_send.at[g, half], bwd_recv.at[g], device)

                @pl.when(low == half)
                def _():
                    pltpu.make_async_copy(moved[g].at[me], back[g].at[me], bwd_recv.at[g]).start()
            else:
                send(moved[g].at[other], back[g].at[me], bwd_send.at[g, half], bwd_recv.at[g], device)

    def finish(g):
        first, last = CHUNKS[g]
        landed(back[g], bwd_recv.at[g])
        matrix = turning_t[...]
        for at, s0 in enumerate(range(first, last, 2)):
            if s0 + 1 == last:
                block = back[g][:, 2 * at].reshape(256, 128)
                block = jnp.concatenate([block[:, :64], block[:, 64:]], axis=0)
                out_ref[s0] = nn(matrix, block).T.astype(jnp.bfloat16)
                continue
            block = jnp.concatenate([back[g][:, 2 * at + h].reshape(256, 128) for h in range(2)], axis=0)
            piece = nn(matrix, block).T.astype(jnp.bfloat16)
            for m in range(2):
                out_ref[s0 + m] = piece[m * 64:(m + 1) * 64]

    loads[3].wait()
    for g in range(count):
        turn(g)
        if g == 0:
            @pl.when(jnp.logical_not(is_first))
            def _():
                pl.semaphore_wait(barrier, len(friends) - jnp.where(knows_first, 1, 0))
        spread(g)

    prepare_steps()
    prepare_return()
    greet_first()
    stages = {
        "b": rise, "a": sink, "y": lambda g: lay(got[g], 128, 4, g), "h": lambda g: translate(g, 1), "l": lambda g: translate(g, 0), "e": finish,
    }
    for token in ORDER:
        stages[token[0]](int(token[1:]))

    for g in range(count):
        landed(turned[g].at[pl.ds(0, 31)], fwd_send.at[g])
        landed(below[g], halo_send.at[g, 0])
        landed(above[g], halo_send.at[g, 1])
        for half in range(2):
            @pl.when(low == half)
            def _():
                landed(moved[g].at[pl.ds(0, 15)], bwd_send.at[g, half])

            @pl.when(low != half)
            def _():
                landed(moved[g].at[pl.ds(0, 16)], bwd_send.at[g, half])

def on_device(multipoles, rotation, coaxial, offsets, class_index):
    tables = jnp.asarray(block_tables(), jnp.bfloat16)
    rows = jnp.transpose(multipoles, (1, 0, 2))
    hbm = pl.BlockSpec(memory_space=pl.ANY)
    count = len(CHUNKS)
    bf16 = jnp.bfloat16
    scratch = []
    for outer in (32, 32, 16, 16, 32, 32):
        scratch += [pltpu.VMEM((outer, tiles(g), 8, 128), bf16) for g in range(count)]
    dma = pltpu.SemaphoreType.DMA
    scratch += [
        pltpu.SMEM((NCLASS * PER,), jnp.int32),
        pltpu.SMEM((NCLASS * PER,), jnp.int32),
        pltpu.VMEM((COMPONENTS, 64, 128), bf16),
        pltpu.VMEM((COMPONENTS, 512, 128), jnp.float32),
        pltpu.VMEM((4, 128, 128), bf16),
        pltpu.VMEM((NCLASS, 1, 128, 128), bf16),
        pltpu.VMEM((NCLASS * PER, 1, 128, 128), bf16),
        pltpu.VMEM((NCLASS * 128, 128), bf16),
        pltpu.VMEM((128, NCLASS * 128), bf16),
        pltpu.VMEM((PER, 128, 128), bf16),
        pltpu.SMEM((PER,), jnp.int32),
        dma((6,)), pltpu.SemaphoreType.REGULAR,
        dma((count,)), dma((count, 2)),
        dma((count, 2)), dma((count, 2)),
        dma((count, 2)), dma((count,)),
    ]
    field = pl.pallas_call(
        kernel,
        out_shape=pltpu.VMEM((COMPONENTS, 64, 128), bf16),
        in_specs=[hbm] * 6,
        out_specs=pl.BlockSpec(memory_space=pltpu.VMEM),
        scratch_shapes=scratch,
        compiler_params=pltpu.CompilerParams(collective_id=0, has_side_effects=True),
        name="multipole_to_local",
    )(rows, tables, rotation, coaxial, offsets, class_index)
    return jnp.transpose(field, (1, 0, 2))


def solution(mesh):
    placed = (
        P("cell", None, "coef"),
        P(None, "coef", None, None),
        P(None, "coef", None, None),
        P(),
        P(),
    )
    return jax.shard_map(
        on_device, mesh=mesh, in_specs=placed, out_specs=P("cell", None, "coef"), check_vma=False
    )
```

```python
import jax
import jax.numpy as jnp
import numpy as np
from jax import lax
from jax.experimental import pallas as pl
from jax.experimental.pallas import tpu as pltpu
from jax.sharding import PartitionSpec as P

NCLASS = 4
PER = 10
COMPONENTS = 9
CHUNKS = ((0, 3), (3, 7), (7, 9))
ORDER = (
    "b0", "a0", "y0", "b1", "a1", "b2", "a2", "y1", "h0", "h1", "l0", "y2", "h2", "l1", "l2", "e0", "e1", "e2",
)
MESH = pl.DeviceIdType.MESH


def far_first():
    ways = {}
    for dx in range(4):
        for dy in range(4):
            for dc in range(2):
                if (dx, dy, dc) != (0, 0, 0):
                    ways.setdefault((dx, dy), []).append((dx, dy, dc))
    hops = lambda way: min(way[0], 4 - way[0]) + min(way[1], 4 - way[1])
    keys = sorted(ways, key=lambda way: -hops(way))
    return [ways[key][-1 - turn] for turn in range(2) for key in keys if turn < len(ways[key])]


FAR_FIRST = far_first()
HALF_FAR_FIRST = [
    (dx, dh, dc) for dc in (1, 0) for dx, dh in (
        (2, 1), (2, 0), (1, 1), (3, 1), (0, 1), (1, 0), (3, 0), (0, 0))]


def block_tables():
    degree_list = []
    for block_number in range(8):
        for level in (block_number, 15 - block_number, 16 + block_number, 31 - block_number):
            for order in range(-level, level + 1):
                degree_list.append((level, order))
    order_list = []
    for block_number in range(8):
        if block_number == 0:
            magnitudes = (0, 16, 8, 24)
        else:
            magnitudes = (block_number, 32 - block_number, 16 - block_number, 16 + block_number)
        for size_m in magnitudes:
            for order in [size_m] if size_m == 0 else [size_m, -size_m]:
                for level in range(size_m, 32):
                    order_list.append((level, order))
    where_degree = {pair: index for index, pair in enumerate(degree_list)}
    by_degree = np.zeros((8, 128, 128), np.float32)
    by_order = np.zeros((8, 128, 128), np.float32)
    filled = np.zeros((8, 8), np.int32)
    for order_at, pair in enumerate(order_list):
        degree_at = where_degree[pair]
        a, b = degree_at // 128, order_at // 128
        slot = filled[a, b]
        filled[a, b] += 1
        by_degree[a, b * 16 + slot, degree_at % 128] = 1.0
        by_order[b, (slot // 8) * 64 + a * 8 + slot % 8, order_at % 128] = 1.0
    assert (filled == 16).all()
    levels = np.array([pair[0] for pair in degree_list]).reshape(8, 128)
    orders = np.array([pair[1] for pair in order_list]).reshape(8, 128)
    same_level = (levels[:, :, None] == levels[:, None, :]).astype(np.float32)
    same_order = (orders[:, :, None] == orders[:, None, :]).astype(np.float32)
    return np.stack([by_degree, by_order, same_level, same_order], axis=1)


def tiles(g):
    return CHUNKS[g][1] - CHUNKS[g][0]


def nt(left, right):
    return lax.dot_general(left, right, (((1,), (1,)), ((), ())), preferred_element_type=jnp.float32)


def nn(left, right):
    return jnp.dot(left, right, preferred_element_type=jnp.float32)


def halves_first(rows):
    count, width = rows.shape[0] // 16, rows.shape[1]
    split = rows.reshape(count, 2, 8, width)
    return jnp.concatenate([split[:, h].reshape(count * 8, width) for h in range(2)], axis=0)


def kernel(x_hbm, tables_hbm, rot_hbm, coax_hbm, offs_hbm, cls_hbm, out_ref, *scratch):
    count = len(CHUNKS)
    names = ("turned", "got", "below", "above", "moved", "back")
    buffers = {name: scratch[i * count:(i + 1) * count] for i, name in enumerate(names)}
    turned, got, below, above, moved, back = (buffers[name] for name in names)
    (offs_ref, cls_ref, x_ref, cells, tables, rot, coax, turning, turning_t, steps, chosen, load_sem, late_sem,
     fwd_send, fwd_recv, halo_send, halo_recv, bwd_send, bwd_recv) = scratch[len(names) * count:]
    cell = lax.axis_index("cell")
    coef = lax.axis_index("coef")
    cell_total = lax.axis_size("cell")
    part = cell % 4
    plane = cell - part
    me = part * 8 + coef
    along, high, low, core = coef % 4, coef // 4, part // 2, part % 2
    up = (cell + 4) % cell_total
    down = (cell + cell_total - 4) % cell_total
    is_first = jnp.logical_and(cell == 0, coef == 0)
    beside_first = jnp.logical_and(coef == 0, jnp.logical_or(up == 0, down == 0))
    knows_first = jnp.logical_and(
        jnp.logical_not(is_first), jnp.logical_or(plane == 0, beside_first))

    xs = [(along + i) % 4 for i in range(4)]
    ys = [(high * 2 + low + i) % 4 for i in range(4)]
    cores = [core, 1 - core]

    def partner(dx, dy, dc):
        to_part = (ys[dy] % 2) * 2 + cores[dc]
        to_coef = (ys[dy] // 2) * 4 + xs[dx]
        return to_part * 8 + to_coef, (plane + to_part, to_coef)

    def half_partner(half, dx, dh, dc):
        to_part = half * 2 + cores[dc]
        to_coef = (high + dh) % 2 * 4 + xs[dx]
        return to_part * 8 + to_coef, (plane + to_part, to_coef)

    barrier = pltpu.get_barrier_semaphore()
    friends = [partner(*step)[1] for step in FAR_FIRST] + [(up, coef), (down, coef)]

    @pl.when(jnp.logical_not(is_first))
    def _():
        for device in friends:
            pl.semaphore_signal(barrier, inc=1, device_id=device, device_id_type=MESH)

    loads = [
        pltpu.make_async_copy(tables_hbm.at[coef], tables, load_sem.at[0]),
        pltpu.make_async_copy(rot_hbm, rot, load_sem.at[1]),
        pltpu.make_async_copy(coax_hbm, coax, load_sem.at[2]),
        pltpu.make_async_copy(x_hbm, x_ref, load_sem.at[3]),
        pltpu.make_async_copy(offs_hbm, offs_ref, load_sem.at[4]),
        pltpu.make_async_copy(cls_hbm, cls_ref, load_sem.at[5]),
    ]
    for load in (loads[0], loads[1], loads[3], loads[2], loads[4], loads[5]):
        load.start()

    @pl.when(is_first)
    def _():
        pl.semaphore_wait(barrier, len(friends))
        for device in friends:
            pl.semaphore_signal(late_sem, inc=1, device_id=device, device_id_type=MESH)

    loads[0].wait()
    loads[1].wait()
    for c in range(NCLASS):
        masked = rot[c, 0] * tables[2]
        turning[c * 128:(c + 1) * 128, :] = nn(tables[0], masked).astype(jnp.bfloat16)

    def send(source, target, send_sem, recv_sem, device):
        pltpu.make_async_remote_copy(
            source, target, send_sem, recv_sem, device_id=device, device_id_type=MESH).start()

    def landed(ref, sem):
        pltpu.make_async_copy(ref, ref, sem).wait()

    def turn(g):
        first, last = CHUNKS[g]
        for at, s0 in enumerate(range(first, last, 2)):
            members = range(s0, min(s0 + 2, last))
            rows = x_ref[s0:members[-1] + 1].reshape(len(members) * 64, 128)
            result = nt(turning[...], rows).reshape(32, 2, 8, len(members) * 64)
            if len(members) == 1:
                result = jnp.concatenate([result[:, 0], result[:, 1]], axis=2)
                turned[g][:, 2 * at] = result.astype(jnp.bfloat16)
            else:
                for h in range(2):
                    turned[g][:, 2 * at + h] = result[:, h].astype(jnp.bfloat16)

    def spread(g):
        def each(guarded):
            for step in FAR_FIRST:
                other, device = partner(*step)
                if guarded:
                    @pl.when(other != 0)
                    def _():
                        send(turned[g].at[other], got[g].at[me], fwd_send.at[g], fwd_recv.at[g, low], device)
                else:
                    send(turned[g].at[other], got[g].at[me], fwd_send.at[g], fwd_recv.at[g, low], device)

        @pl.when(plane != 0)
        def _():
            each(False)

        @pl.when(plane == 0)
        def _():
            each(True)

        pltpu.make_async_copy(turned[g].at[me], got[g].at[me], fwd_recv.at[g, low]).start()

    def greet_first():
        @pl.when(knows_first)
        def _():
            pl.semaphore_wait(late_sem, 1)

        @pl.when(jnp.logical_and(knows_first, plane == 0))
        def _():
            for g in range(count):
                send(turned[g].at[0], got[g].at[me], fwd_send.at[g], fwd_recv.at[g, low], (0, 0))

    def pick(k, carry):
        seen, kept = carry[0], carry[1:]
        hit = cls_ref[k] == part
        kept = tuple(
            jnp.where(jnp.logical_and(hit, seen == p), k, old) for p, old in enumerate(kept))
        return (seen + jnp.where(hit, 1, 0),) + kept

    def prepare_steps():
        loads[4].wait()
        loads[5].wait()
        picked = lax.fori_loop(0, NCLASS * PER, pick, (jnp.int32(0),) * (PER + 1))[1:]
        for p in range(PER):
            chosen[p] = picked[p]
        loads[2].wait()

        def prepare(p, carry):
            masked = coax[chosen[p], 0] * tables[3]
            half = nn(tables[1], masked).astype(jnp.bfloat16)
            steps[p] = nt(half, tables[1]).astype(jnp.bfloat16)
            return carry

        lax.fori_loop(0, PER, prepare, 0)

    def prepare_return():
        rows = halves_first(turning[...].astype(jnp.float32))
        for c in range(NCLASS):
            turning_t[:, c * 128:(c + 1) * 128] = rows[c * 128:(c + 1) * 128].T.astype(jnp.bfloat16)

    def lay(buffer, row, groups, g):
        first, last = CHUNKS[g]
        for j in range(groups):
            for at, s0 in enumerate(range(first, last, 2)):
                if s0 + 1 == last:
                    block = buffer[j * 8:(j + 1) * 8, 2 * at].astype(jnp.float32).reshape(64, 128).T
                    cells[s0, row + j * 64:row + j * 64 + 64, :] = jnp.concatenate(
                        [block[:64], block[64:]], axis=1)
                    continue
                block = jnp.concatenate(
                    [buffer[j * 8:(j + 1) * 8, 2 * at + h].astype(jnp.float32).reshape(64, 128)
                     for h in range(2)], axis=0).T
                for m in range(2):
                    cells[s0 + m, row + j * 64:row + j * 64 + 64, :] = block[m * 64:(m + 1) * 64]

    def rise(g):
        upper = got[g].at[pl.ds(16, 16)]
        landed(upper, fwd_recv.at[g, 1])
        send(upper, below[g], halo_send.at[g, 0], halo_recv.at[g, 0], (up, coef))

    def sink(g):
        lower = got[g].at[pl.ds(0, 16)]
        landed(lower, fwd_recv.at[g, 0])
        send(lower, above[g], halo_send.at[g, 1], halo_recv.at[g, 1], (down, coef))

    def translate(g, half):
        first, last = CHUNKS[g]
        if half:
            landed(above[g], halo_recv.at[g, 1])
            lay(above[g], 384, 2, g)
        else:
            landed(below[g], halo_recv.at[g, 0])
            lay(below[g], 0, 2, g)
        matrices = jnp.concatenate([steps[p] for p in range(PER)], axis=1)
        starts = [128 + half * 128 + offs_ref[chosen[p]] for p in range(PER)]
        for at, s0 in enumerate(range(first, last, 2)):
            members = range(s0, min(s0 + 2, last))
            width = 64 * len(members)
            pieces = []
            for p in range(PER):
                pieces.append(jnp.concatenate(
                    [cells[s, pl.ds(starts[p] + i * 64, 64), :] for i in range(2) for s in members],
                    axis=0).astype(jnp.bfloat16))
            result = nt(matrices, jnp.concatenate(pieces, axis=1))
            for i in range(2):
                row = (half * 2 + i) * 8
                piece = result[:, i * width:(i + 1) * width]
                if len(members) == 1:
                    piece = jnp.concatenate([piece[:64], piece[64:]], axis=1)
                    moved[g][row:row + 8, 2 * at] = piece.reshape(8, 8, 128).astype(jnp.bfloat16)
                else:
                    for h in range(2):
                        moved[g][row:row + 8, 2 * at + h] = (
                            piece[h * 64:(h + 1) * 64].reshape(8, 8, 128).astype(jnp.bfloat16))
        for step in HALF_FAR_FIRST:
            other, device = half_partner(half, *step)
            if step == (0, 0, 0):
                @pl.when(low != half)
                def _():
                    send(moved[g].at[other], back[g].at[me], bwd_send.at[g, half], bwd_recv.at[g], device)

                @pl.when(low == half)
                def _():
                    pltpu.make_async_copy(moved[g].at[me], back[g].at[me], bwd_recv.at[g]).start()
            else:
                send(moved[g].at[other], back[g].at[me], bwd_send.at[g, half], bwd_recv.at[g], device)

    def finish(g):
        first, last = CHUNKS[g]
        landed(back[g], bwd_recv.at[g])
        matrix = turning_t[...]
        for at, s0 in enumerate(range(first, last, 2)):
            if s0 + 1 == last:
                block = back[g][:, 2 * at].reshape(256, 128)
                block = jnp.concatenate([block[:, :64], block[:, 64:]], axis=0)
                out_ref[s0] = nn(matrix, block).T.astype(jnp.bfloat16)
                continue
            block = jnp.concatenate([back[g][:, 2 * at + h].reshape(256, 128) for h in range(2)], axis=0)
            piece = nn(matrix, block).T.astype(jnp.bfloat16)
            for m in range(2):
                out_ref[s0 + m] = piece[m * 64:(m + 1) * 64]

    loads[3].wait()
    for g in range(count):
        turn(g)
        if g == 0:
            @pl.when(jnp.logical_not(is_first))
            def _():
                pl.semaphore_wait(barrier, len(friends) - jnp.where(knows_first, 1, 0))
        spread(g)

    prepare_steps()
    prepare_return()
    greet_first()
    stages = {
        "b": rise, "a": sink, "y": lambda g: lay(got[g], 128, 4, g), "h": lambda g: translate(g, 1), "l": lambda g: translate(g, 0), "e": finish,
    }
    for token in ORDER:
        stages[token[0]](int(token[1:]))

    for g in range(count):
        landed(turned[g].at[pl.ds(0, 31)], fwd_send.at[g])
        landed(below[g], halo_send.at[g, 0])
        landed(above[g], halo_send.at[g, 1])
        for half in range(2):
            @pl.when(low == half)
            def _():
                landed(moved[g].at[pl.ds(0, 15)], bwd_send.at[g, half])

            @pl.when(low != half)
            def _():
                landed(moved[g].at[pl.ds(0, 16)], bwd_send.at[g, half])

def on_device(multipoles, rotation, coaxial, offsets, class_index):
    tables = jnp.asarray(block_tables(), jnp.bfloat16)
    rows = jnp.transpose(multipoles, (1, 0, 2))
    hbm = pl.BlockSpec(memory_space=pl.ANY)
    count = len(CHUNKS)
    bf16 = jnp.bfloat16
    scratch = []
    for outer in (32, 32, 16, 16, 32, 32):
        scratch += [pltpu.VMEM((outer, tiles(g), 8, 128), bf16) for g in range(count)]
    dma = pltpu.SemaphoreType.DMA
    scratch += [
        pltpu.SMEM((NCLASS * PER,), jnp.int32),
        pltpu.SMEM((NCLASS * PER,), jnp.int32),
        pltpu.VMEM((COMPONENTS, 64, 128), bf16),
        pltpu.VMEM((COMPONENTS, 512, 128), jnp.float32),
        pltpu.VMEM((4, 128, 128), bf16),
        pltpu.VMEM((NCLASS, 1, 128, 128), bf16),
        pltpu.VMEM((NCLASS * PER, 1, 128, 128), bf16),
        pltpu.VMEM((NCLASS * 128, 128), bf16),
        pltpu.VMEM((128, NCLASS * 128), bf16),
        pltpu.VMEM((PER, 128, 128), bf16),
        pltpu.SMEM((PER,), jnp.int32),
        dma((6,)), pltpu.SemaphoreType.REGULAR,
        dma((count,)), dma((count, 2)),
        dma((count, 2)), dma((count, 2)),
        dma((count, 2)), dma((count,)),
    ]
    field = pl.pallas_call(
        kernel,
        out_shape=pltpu.VMEM((COMPONENTS, 64, 128), bf16),
        in_specs=[hbm] * 6,
        out_specs=pl.BlockSpec(memory_space=pltpu.VMEM),
        scratch_shapes=scratch,
        compiler_params=pltpu.CompilerParams(collective_id=0, has_side_effects=True),
        name="multipole_to_local",
    )(rows, tables, rotation, coaxial, offsets, class_index)
    return jnp.transpose(field, (1, 0, 2))


def solution(mesh):
    placed = (
        P("cell", None, "coef"),
        P(None, "coef", None, None),
        P(None, "coef", None, None),
        P(),
        P(),
    )
    return jax.shard_map(
        on_device, mesh=mesh, in_specs=placed, out_specs=P("cell", None, "coef"), check_vma=False
    )
```
